256 devices in a mesh: ctx: 32 (over z, x), head: 8 (over y, core).
Axes of the slice: x: 4, y: 4, z: 8, core: 2. Of those that a mesh axis runs over, the one named last changes fastest.
Arguments:
- lin_query: bfloat16 [12288, 8192], P('ctx', 'head'), may hold values from -4 to 4
- lin_key: bfloat16 [12288, 8192], P('ctx', 'head'), may hold values from -4 to 4
- lin_value: bfloat16 [12288, 8192], P('ctx', 'head'), may hold values from -400 to 400
- lin_gate: bfloat16 [12288, 8192], P('ctx', 'head'), may hold values from -8 to 8
- lin_decay: float32 [12288, 64], P('ctx', 'head'), may hold values from -1 to 0
- norm_gain: float32 [8192], P('head'), may hold values from 0.25 to 1.75
- soft_query: bfloat16 [12288, 8192], P('ctx', 'head'), may hold values from -6.5 to 6.5
- soft_key: bfloat16 [12288, 1024], P('ctx', 'head'), may hold values from -6.5 to 6.5
- soft_value: bfloat16 [12288, 1024], P('ctx', 'head'), may hold values from -6 to 6
- starts: int32 [4], replicated, may hold values from 1 to 9408, as said below
- lengths: int32 [4], replicated, may hold values from 1536 to 3072, as said below
Outputs:
- lin_out: bfloat16 [12288, 8192], P('ctx', 'head')
- soft_out: bfloat16 [12288, 8192], P('ctx', 'head')
The draws below stay inside these ranges and needn't reach their ends.
Inputs may be any that keep to these rules, and one draw needn't show every extreme that they name: `starts`: sequence s begins 1 to min(384, 192) positions after s * 3072; sequences 1 and 2 begin at the same offset, no sequence runs into the next, and the last one ends at the pack's end. `lengths`: sequence 1 has length 3072 in every draw.
All inputs are finite; a program needn't handle non-finite values.
Results may differ from the reference program's by a relative error of at most 0.012.
Values may be sent and summed in bfloat16 or wider, within the bound.
No kernel may reach another device: no remote copies, remote signals or barrier semaphores. Data moves between devices by JAX's collectives and lax.ppermute only.
A program may use at most 128 MiB of HBM per device.

```python
import math
import jax
import jax.numpy as jnp
from jax import lax

HEADS = 64
HD = 128
KV_HEADS = 8
TOK_DEV = 384
SEQS = 4
WIDTH = 8192
KV_WIDTH = 1024
PACK_LENGTH = 12288
SEQUENCE_ROOM = 3072
KEY_SPAN = 3456


def sequence_bounds(key):
    floor_level = jax.random.fold_in(key, 29)
    key_offset, key_length = jax.random.split(floor_level, 2)
    slot_ids = jnp.arange(SEQS, dtype=jnp.int32)
    top_offset = min(SEQUENCE_ROOM // 8, TOK_DEV // 2)
    offsets = jax.random.randint(key_offset, (SEQS,), 1, top_offset + 1)
    offsets = jnp.where(slot_ids == 2, offsets[1], offsets)
    first = slot_ids * SEQUENCE_ROOM + offsets
    following = jnp.concatenate([first[1:], jnp.array([PACK_LENGTH], dtype=jnp.int32)])
    room_left = following - first
    length_top = jnp.minimum(room_left, SEQUENCE_ROOM)
    chosen = jax.random.randint(key_length, (SEQS,), SEQUENCE_ROOM // 2, length_top + 1)
    chosen = jnp.where(slot_ids == 1, SEQUENCE_ROOM, chosen)
    chosen = jnp.where(slot_ids == SEQS - 1, room_left, chosen)
    return (first.astype(jnp.int32), chosen.astype(jnp.int32))


def draw_starts(key, part):
    first, unused = sequence_bounds(key)
    return first


def draw_lengths(key, part):
    unused, chosen = sequence_bounds(key)
    return chosen


def draw_lin_decay(key, part):
    floor_level = jax.random.fold_in(key, 3)
    quick_seed, speed_seed, gradual_seed, noise_seed, spike_seed, drop_seed = jax.random.split(floor_level, 6)
    fast_share = 0.5
    fast = jax.random.uniform(quick_seed, (HEADS,)) < fast_share
    fast_rate = jnp.exp(jax.random.uniform(speed_seed, (HEADS,), minval=math.log(0.05), maxval=math.log(0.1)))
    slow_rate = jnp.exp(jax.random.uniform(gradual_seed, (HEADS,), minval=math.log(0.05), maxval=math.log(0.5))) / SEQUENCE_ROOM
    forget_factor = jnp.where(fast, fast_rate, slow_rate)
    noise_size = jax.random.uniform(noise_seed, (PACK_LENGTH, HEADS), minval=0.5, maxval=1.5)
    spike_size = jax.random.randint(spike_seed, (PACK_LENGTH, 1), 0, SEQUENCE_ROOM // 2) == 0
    drop_size = jax.random.uniform(drop_seed, (PACK_LENGTH, HEADS), minval=0.2, maxval=0.5)
    element_item = -forget_factor[None, :] * noise_size + jnp.where(spike_size, jnp.log(1.0 - drop_size), 0.0)
    return element_item.astype(jnp.float32)


def draw_lin_value(key, part):
    floor_level = jax.random.fold_in(key, 5)
    key_base, key_column, key_row = jax.random.split(floor_level, 3)
    features = HEADS * HD
    head_of = (jnp.arange(features) // HD).astype(jnp.float32)
    ramp = jnp.power(3.0, head_of / max(HEADS - 1, 1))
    column_scale = ramp * jnp.exp(jax.random.uniform(key_column, (features,), minval=0.0, maxval=math.log(3.3)))
    entries = jnp.clip(jax.random.normal(key_base, (PACK_LENGTH, features)), -4.0, 4.0)
    row_scale = jnp.exp(jax.random.uniform(key_row, (PACK_LENGTH, 1), minval=0.0, maxval=math.log(10.0)))
    return (entries * column_scale[None, :] * row_scale).astype(jnp.bfloat16)


def soft_pair(key):
    floor_level = jax.random.fold_in(key, 17)
    key_query, key_key = jax.random.split(floor_level, 2)
    features = HEADS * HD
    kv_features = KV_HEADS * HD
    queries = jnp.clip(jax.random.normal(key_query, (PACK_LENGTH, features)), -4.0, 4.0)
    keys = jnp.clip(jax.random.normal(key_key, (PACK_LENGTH, kv_features)), -4.0, 4.0)
    return (queries, keys)


def draw_soft_query(key, part):
    queries, keys = soft_pair(key)
    return queries.astype(jnp.bfloat16)


def draw_soft_key(key, part):
    queries, keys = soft_pair(key)
    return keys.astype(jnp.bfloat16)


def shard_levels(key, extent, cuts, low, top_value):
    level, own = 1.0, jax.random.fold_in(key, 6)
    for position, shards_of in cuts:
        heights = jnp.exp(jax.random.uniform(jax.random.fold_in(own, position), (shards_of,), jnp.float32, low / len(cuts), top_value / len(cuts)))
        level = level * jnp.repeat(heights, extent[position] // shards_of).reshape([-1 if axis == position else 1 for axis in range(len(extent))])
    return level


def noise(rng, extent, scale, most, shards=(), kind=jnp.bfloat16):
    values = jax.random.normal(rng, extent, jnp.float32) * scale
    if len(shards) > 0:
        values = shard_levels(rng, extent, shards, -0.22, 0.18) * values
    return jnp.clip(values, min=-most, max=most).astype(kind)


def setup_inputs(seed: int = 0) -> dict:
    seeds = jax.random.split(jax.random.key(seed), 12)
    lin_query = noise(seeds[0], (PACK_LENGTH, WIDTH), 1.0, 4.0, ((0, 32), (1, 8)))
    lin_key = noise(seeds[1], (PACK_LENGTH, WIDTH), 1.0, 4.0, ((0, 32), (1, 8)))
    lin_value = draw_lin_value(jax.random.fold_in(seeds[11], 71), 0)
    lin_gate = noise(seeds[3], (PACK_LENGTH, WIDTH), 2.0, 8.0, ((0, 32), (1, 8)))
    lin_decay = draw_lin_decay(jax.random.fold_in(seeds[11], 71), 0)
    norm_gain = jnp.clip(1.0 + 0.15 * jax.random.normal(seeds[5], (WIDTH,), jnp.float32), 0.25, 1.75)
    soft_query = draw_soft_query(jax.random.fold_in(seeds[11], 71), 0)
    soft_key = draw_soft_key(jax.random.fold_in(seeds[11], 71), 0)
    soft_value = noise(seeds[8], (PACK_LENGTH, KV_WIDTH), 1.0, 6.0, ((0, 32), (1, 8)))
    starts = draw_starts(jax.random.fold_in(seeds[11], 71), 0)
    lengths = draw_lengths(jax.random.fold_in(seeds[11], 71), 0)
    return {"lin_query": lin_query, "lin_key": lin_key, "lin_value": lin_value, "lin_gate": lin_gate, "lin_decay": lin_decay, "norm_gain": norm_gain, "soft_query": soft_query, "soft_key": soft_key, "soft_value": soft_value, "starts": starts, "lengths": lengths}


neg_big = -1e+30
norm_eps = 1e-06

def segment_info(positions, starts, lengths):
    begun = (starts[None, :] <= positions[:, None]).astype(jnp.int32)
    segment = lax.optimization_barrier(jnp.sum(begun, axis=1)) - 1
    picked = jnp.arange(starts.shape[0], dtype=jnp.int32)[None, :] == segment[:, None]
    seg_start = lax.optimization_barrier(jnp.sum(jnp.where(picked, starts[None, :], 0), axis=1))
    seg_length = lax.optimization_barrier(jnp.sum(jnp.where(picked, lengths[None, :], 0), axis=1))
    valid = (segment >= 0) & (positions < seg_start + seg_length)
    return (segment, valid)

def lightning_local(query, keys, values, decay, segment, valid, before):
    row_count = query.shape[0]
    cumulative = jnp.cumsum(decay, axis=0)
    row_order = jnp.arange(row_count)
    visible = (row_order[None, :] <= row_order[:, None]) & (segment[None, :] == segment[:, None]) & valid[None, :]
    by_head = jnp.transpose(cumulative)
    log_gap = by_head[:, :, None] - by_head[:, None, :]
    factor = jnp.where(visible[None], jnp.exp(jnp.where(visible[None], log_gap, 0.0)), 0.0)
    scores = jnp.einsum('thd,shd->hts', query.astype(jnp.float32), keys.astype(jnp.float32), precision=lax.Precision.HIGHEST)
    weights = (scores * factor).astype(jnp.bfloat16)
    intra = jnp.einsum('hts,shd->thd', weights.astype(jnp.float32), values.astype(jnp.float32), precision=lax.Precision.HIGHEST)
    enter = jnp.exp(cumulative) * (segment == before).astype(jnp.float32)[:, None]
    end_ok = ((segment == segment[-1]) & valid).astype(jnp.float32)
    to_end = jnp.exp(cumulative[-1][None, :] - cumulative) * end_ok[:, None]
    decay_total = jnp.exp(cumulative[-1]) * (segment[-1] == before).astype(jnp.float32)
    local_state = jnp.einsum('thd,the->hde', keys.astype(jnp.float32) * to_end[:, :, None], values.astype(jnp.float32), precision=lax.Precision.HIGHEST)
    return (intra, enter, decay_total, local_state)

def reference(lin_query, lin_key, lin_value, lin_gate, lin_decay, norm_gain, soft_query, soft_key, soft_value, starts, lengths):
    blocks = PACK_LENGTH // TOK_DEV
    group = HEADS // KV_HEADS

    def blocked(array):
        return array.reshape(blocks, TOK_DEV, HEADS, HD)

    def lightning_step(state, inputs):
        block_index, query, keys, values, decay = inputs
        first = block_index * TOK_DEV
        positions = first + jnp.arange(TOK_DEV, dtype=jnp.int32)
        segment, valid = segment_info(positions, starts, lengths)
        before, unused = segment_info(jnp.reshape(first - 1, (1,)), starts, lengths)
        intra, enter, decay_total, local_state = lightning_local(query, keys, values, decay, segment, valid, before[0])
        carried = jnp.einsum('thd,hde->the', query.astype(jnp.float32) * enter[:, :, None], state, precision=lax.Precision.HIGHEST)
        heads_out = (intra + carried) * valid.astype(jnp.float32)[:, None, None]
        new_state = decay_total[:, None, None] * state + local_state
        return (new_state, heads_out)
    initial = jnp.zeros((HEADS, HD, HD), jnp.float32)
    indices = jnp.arange(blocks, dtype=jnp.int32)
    decays = lin_decay.reshape(blocks, TOK_DEV, HEADS)
    unused_state, lin_heads = lax.scan(lightning_step, initial, (indices, blocked(lin_query), blocked(lin_key), blocked(lin_value), decays))
    flat = lin_heads.reshape(PACK_LENGTH, HEADS * HD)
    mean_square = lax.optimization_barrier(jnp.mean(flat * flat, axis=1))
    lin_out = (flat * lax.rsqrt(mean_square + norm_eps)[:, None] * norm_gain[None, :] * jax.nn.sigmoid(lin_gate.astype(jnp.float32))).astype(jnp.bfloat16)
    positions_all = jnp.arange(PACK_LENGTH, dtype=jnp.int32)
    seg_all, valid_all = segment_info(positions_all, starts, lengths)
    score_scale = HD ** (-0.5)
    query_heads = jnp.transpose(soft_query.reshape(PACK_LENGTH, KV_HEADS, group, HD), (1, 2, 0, 3))
    key_heads = jnp.transpose(soft_key.reshape(PACK_LENGTH, KV_HEADS, HD), (1, 0, 2))
    value_heads = jnp.transpose(soft_value.reshape(PACK_LENGTH, KV_HEADS, HD), (1, 0, 2))

    def soft_block(block_index):
        first = (block_index * TOK_DEV).astype(jnp.int32)
        key_first = jnp.clip(first - SEQUENCE_ROOM, 0, PACK_LENGTH - KEY_SPAN).astype(jnp.int32)
        query_seg = lax.dynamic_slice_in_dim(seg_all, first, TOK_DEV, 0)
        query_valid = lax.dynamic_slice_in_dim(valid_all, first, TOK_DEV, 0)
        key_seg = lax.dynamic_slice_in_dim(seg_all, key_first, KEY_SPAN, 0)
        key_valid = lax.dynamic_slice_in_dim(valid_all, key_first, KEY_SPAN, 0)
        query_pos = first + jnp.arange(TOK_DEV, dtype=jnp.int32)
        key_pos = key_first + jnp.arange(KEY_SPAN, dtype=jnp.int32)
        visible = (key_pos[None, :] <= query_pos[:, None]) & (key_seg[None, :] == query_seg[:, None]) & key_valid[None, :]
        query_block = lax.dynamic_slice_in_dim(query_heads, first, TOK_DEV, 2)
        key_block = lax.dynamic_slice_in_dim(key_heads, key_first, KEY_SPAN, 1)
        value_block = lax.dynamic_slice_in_dim(value_heads, key_first, KEY_SPAN, 1)

        def one_head(operands):
            query_one, key_one, value_one = operands
            scores = jnp.einsum('gqd,sd->gqs', query_one.astype(jnp.float32), key_one.astype(jnp.float32), precision=lax.Precision.HIGHEST) * score_scale
            masked = jnp.where(visible[None], scores, neg_big)
            peak = lax.optimization_barrier(jnp.max(masked, axis=2, keepdims=True))
            probs = jnp.where(visible[None], jnp.exp(masked - peak), 0.0)
            totals = lax.optimization_barrier(jnp.sum(probs, axis=2, keepdims=True))
            mixed = jnp.einsum('gqs,sd->gqd', probs.astype(jnp.bfloat16).astype(jnp.float32), value_one.astype(jnp.float32), precision=lax.Precision.HIGHEST)
            safe = jnp.where(query_valid[None, :, None], totals, 1.0)
            return (mixed / safe * query_valid.astype(jnp.float32)[None, :, None]).astype(jnp.bfloat16)
        return lax.map(one_head, (query_block, key_block, value_block))
    soft_heads = lax.map(soft_block, jnp.arange(blocks, dtype=jnp.int32))
    soft_out = jnp.transpose(soft_heads, (0, 3, 1, 2, 4)).reshape(PACK_LENGTH, HEADS * HD)
    return (lin_out, soft_out)
```

```python
import functools
import jax
import jax.numpy as jnp
from jax import lax
from jax.experimental import pallas as pl
from jax.experimental.pallas import tpu as pltpu
from jax.sharding import PartitionSpec as P


T = 384
D = 128
H = 8
SPAN = 8
NEG = -1e30
EPS = 1e-06
GONE = -1e5
EXTRA = 32
HI = lax.Precision.HIGHEST
F32 = jnp.float32
BF16 = jnp.bfloat16
NT = (((1,), (1,)), ((), ()))
TN = (((0,), (0,)), ((), ()))


def iota(shape, axis):
    return lax.broadcasted_iota(jnp.int32, shape, axis)


def marks(starts, lengths):
    device = lax.axis_index("ctx")
    room = device // SPAN
    place = device % SPAN
    first = device * T
    at_start = place == 0
    bound = jnp.where(at_start, starts[room] - first, 0)
    earlier = jnp.maximum(room - 1, 0)
    end_prev = jnp.where(at_start & (room > 0), starts[earlier] + lengths[earlier] - first, 0)
    end_cur = starts[room] + lengths[room] - first
    return room, place, bound, end_prev, end_cur


def valid_rows(shape, bound, end_prev, end_cur):
    rows = iota(shape, 0)
    return rows < jnp.where(rows < bound, end_prev, end_cur)


def column(table, head):
    lanes = iota(table.shape, 1)
    return jnp.sum(jnp.where(lanes == head, table, 0.0), axis=1, keepdims=True)


def split3(x):
    a = x.astype(BF16)
    rest = x - a.astype(F32)
    b = rest.astype(BF16)
    c = (rest - b.astype(F32)).astype(BF16)
    return a, b, c


def state_kernel(starts, lengths, key, value, decay, pack, cum, cum_t, totals):
    head = pl.program_id(0)
    room, place, bound, end_prev, end_cur = marks(starts, lengths)

    @pl.when(head == 0)
    def _():
        lower = (iota((T, T), 1) <= iota((T, T), 0)).astype(F32)
        dec = decay[...]
        cum[...] = lax.dot_general(lower, dec, (((1,), (0,)), ((), ())), precision=HI,
                                   preferred_element_type=F32)
        cum_t[...] = lax.dot_general(dec, lower, (((0,), (1,)), ((), ())), precision=HI,
                                     preferred_element_type=F32)

    own = column(cum[...], head)
    last = own[T - 1:T, :]
    rows = iota((T, 1), 0)
    keep = (rows >= bound) & (rows < end_cur)
    to_end = jnp.where(keep, jnp.exp(last - own), 0.0)
    scaled = (key[...].astype(F32) * to_end).astype(BF16)
    state = lax.dot_general(scaled, value[...], TN, preferred_element_type=F32)
    pack[pl.ds(pl.multiple_of(head * D, D), D), :] = state.astype(BF16)
    total = jnp.where(place == 0, GONE, last)
    totals[pl.ds(head, 1), :] = jnp.broadcast_to(total, (1, D))

    @pl.when(head == H - 1)
    def _():
        a, b, c = split3(totals[...])
        both = jnp.concatenate([a, b], axis=0)
        rest = jnp.concatenate([c, jnp.zeros_like(c)], axis=0)
        pack[pl.ds(H * D, 16), :] = both
        pack[pl.ds(H * D + 16, 16), :] = rest


def combine_kernel(r1, r2, r3, r4, near, near_low, across):
    def total(ref):
        both = ref[pl.ds(H * D, 16), :].astype(F32)
        rest = ref[pl.ds(H * D + 16, 16), :].astype(F32)
        return both[0:8] + both[8:16] + rest[0:8]

    s1 = total(r1)
    s2 = s1 + total(r2)
    s3 = s2 + total(r3)
    s4 = s3 + total(r4)
    w2, w3, w4 = jnp.exp(s1), jnp.exp(s2), jnp.exp(s3)
    across[...] = jnp.exp(s4)
    for h in range(H):
        part = pl.ds(h * D, D)
        row = slice(h, h + 1)
        state = (r1[part, :].astype(F32) + w2[row] * r2[part, :].astype(F32)
                 + w3[row] * r3[part, :].astype(F32) + w4[row] * r4[part, :].astype(F32))
        near[part, :] = state
        near_low[part, :] = state.astype(BF16)


def intra_kernel(starts, lengths, query, key, value, cum, cum_t, out, bias):
    head = pl.program_id(0)
    room, place, bound, end_prev, end_cur = marks(starts, lengths)

    @pl.when(head == 0)
    def _():
        t = iota((T, T), 0)
        i = iota((T, T), 1)
        seen = (i <= t) & ((i >= bound) | (t < bound))
        bias[...] = jnp.where(seen, 0.0, NEG)

    col = column(cum[...], head)
    row = cum_t[pl.ds(head, 1), :]
    for r in range(T // D):
        part = slice(r * D, (r + 1) * D)
        wide = (r + 1) * D
        scores = lax.dot_general(query[part, :], key[0:wide, :], NT, preferred_element_type=F32)
        gap = (col[part, :] - row[:, 0:wide]) + bias[part, 0:wide]
        weights = (scores * jnp.exp(gap)).astype(BF16)
        out[part, :] = jnp.dot(weights, value[0:wide, :], preferred_element_type=F32)


def carry_kernel(starts, lengths, query, intra, near, far, across, cum, out, squares, acc):
    head = pl.program_id(0)
    room, place, bound, end_prev, end_cur = marks(starts, lengths)

    @pl.when(head == 0)
    def _():
        acc[...] = jnp.zeros_like(acc)

    state = near[...] + across[pl.ds(head, 1), :] * far[...].astype(F32)
    high = state.astype(BF16)
    low = (state - high.astype(F32)).astype(BF16)
    q = query[...]
    carried = (jnp.dot(q, high, preferred_element_type=F32)
               + jnp.dot(q, low, preferred_element_type=F32))
    rows = iota((T, 1), 0)
    enters = (place > 0) | (rows < bound)
    enter = jnp.where(enters, jnp.exp(column(cum[...], head)), 0.0)
    valid = valid_rows((T, 1), bound, end_prev, end_cur)
    heads = jnp.where(valid, intra[...] + enter * carried, 0.0)
    out[...] = heads
    acc[...] += heads * heads

    @pl.when(head == H - 1)
    def _():
        squares[...] = lax.dot_general(jnp.ones((8, D), F32), acc[...], NT, precision=HI,
                                       preferred_element_type=F32)


def norm_kernel(heads, gate, gain, squares, out, scale, *, features):
    @pl.when(pl.program_id(0) == 0)
    def _():
        pick = (iota((8, D), 0) == 0).astype(F32)
        sums = lax.dot_general(squares[...], pick, TN, precision=HI, preferred_element_type=F32)
        scale[...] = lax.rsqrt(sums * (1.0 / features) + EPS)

    gated = jax.nn.sigmoid(gate[...].astype(F32))
    out[...] = (heads[...] * scale[...] * gain[...] * gated).astype(BF16)


def soft_kernel(starts, lengths, query, own, f1, f2, f3, f4, f5, f6, f7, f8, out,
                keys, values, bias, scores, top, acc):
    head = pl.program_id(0)
    room, place, bound, end_prev, end_cur = marks(starts, lengths)
    tail = place == 0
    count = jnp.where(tail, jnp.where(room > 0, SPAN, 0), place)
    begin_room = jnp.where(tail, jnp.maximum(room - 1, 0), room)
    begin = starts[begin_room] - begin_room * SPAN * T
    factor = (D ** -0.5) * 1.4426950408889634

    @pl.when(head == 0)
    def _():
        t = iota((T, T), 0)
        i = iota((T, T), 1)
        seen = (i <= t) & ((i >= bound) | (t < bound))
        bias[...] = jnp.where(seen, 0.0, NEG)
        ones = jnp.ones((T, D), BF16)
        for m, ref in enumerate((own, f1, f2, f3, f4, f5, f6, f7, f8)):
            @pl.when(m <= count)
            def _():
                keys[m] = ref[:, 0:D]
                values[m, :, 0:D] = ref[:, D:2 * D]
                values[m, :, D:2 * D] = ones

    def lanes_max(x):
        best = x[:, 0:D]
        for j in range(1, T // D):
            best = jnp.maximum(best, x[:, j * D:(j + 1) * D])
        return best

    first = lax.dot_general(query[...], keys[0], NT, preferred_element_type=F32) + bias[...]
    scores[0] = first
    top[...] = lanes_max(first)

    def score_far(size):
        def middle(m, _):
            x = lax.dot_general(query[0:size, :], keys[m], NT, preferred_element_type=F32)
            scores[m, 0:size, :] = x
            top[0:size, :] = jnp.maximum(top[0:size, :], lanes_max(x))
            return 0

        lax.fori_loop(1, count, middle, 0)
        x = lax.dot_general(query[0:size, :], keys[count], NT, preferred_element_type=F32)
        hidden = iota((size, T), 1) < begin
        if size < T:
            hidden = hidden | (iota((size, T), 0) >= bound)
        x = jnp.where(hidden, NEG, x)
        scores[count, 0:size, :] = x
        top[0:size, :] = jnp.maximum(top[0:size, :], lanes_max(x))

    half = T // 2

    def score_tail():
        far_rows = iota((half, T), 0) < bound
        far_keys = iota((half, T), 1) >= begin

        def one(m, _):
            x = lax.dot_general(query[0:half, :], keys[m], NT, preferred_element_type=F32)
            x = jnp.where(far_rows & (far_keys | (m < count)), x, NEG)
            scores[m, 0:half, :] = x
            top[0:half, :] = jnp.maximum(top[0:half, :], lanes_max(x))
            return 0

        lax.fori_loop(1, count + 1, one, 0)

    pl.when(place > 0)(lambda: score_far(T))
    pl.when(tail & (count > 0))(score_tail)

    peak = jnp.max(top[...], axis=1, keepdims=True) * factor
    top[...] = jnp.broadcast_to(peak, (T, D))

    def weigh(m, size):
        high = top[0:size, 0:1]
        p = jnp.exp2(scores[m, 0:size, :] * factor - high).astype(BF16)
        return jnp.dot(p, values[m], preferred_element_type=F32)

    acc[...] = weigh(0, T)

    def mix_far(size):
        def one(m, _):
            acc[0:size, :] += weigh(m, size)
            return 0

        lax.fori_loop(1, count + 1, one, 0)

    pl.when(place > 0)(lambda: mix_far(T))
    pl.when(tail & (count > 0))(lambda: mix_far(half))

    valid = valid_rows((T, 1), bound, end_prev, end_cur)
    mixed = acc[:, 0:D] / acc[:, D:2 * D]
    out[...] = jnp.where(valid, mixed, 0.0).astype(BF16)


smem = pl.BlockSpec(memory_space=pltpu.SMEM)


def per_head(rows=T):
    return pl.BlockSpec((rows, D), lambda h: (0, h))


def whole(*shape):
    return pl.BlockSpec(shape, lambda h: (0,) * len(shape))


def shape(*dims, kind=F32):
    return jax.ShapeDtypeStruct(dims, kind)


def window(distance, rooms):
    pairs = []
    for room in range(rooms):
        base = room * SPAN
        for i in range(base, base + SPAN):
            j = i + distance
            if j <= base + SPAN and j < rooms * SPAN:
                pairs.append((i, j))
    return pairs


def per_device(lin_query, lin_key, lin_value, lin_gate, lin_decay, norm_gain,
               soft_query, soft_key, soft_value, starts, lengths):
    rooms = lax.axis_size("ctx") // SPAN
    share = lax.axis_size("head")
    width = H * D
    send = lambda x, pairs: lax.ppermute(x, "ctx", pairs)

    pack, cum, cum_t = pl.pallas_call(
        state_kernel, grid=(H,),
        in_specs=[smem, smem, per_head(), per_head(), whole(T, H)],
        out_specs=[whole(width + EXTRA, D), whole(T, H), whole(H, T)],
        out_shape=[shape(width + EXTRA, D, kind=BF16), shape(T, H), shape(H, T)],
        scratch_shapes=[pltpu.VMEM((H, D), F32)], name="state",
    )(starts, lengths, lin_key, lin_value, lin_decay)
    states = [send(pack, window(m, rooms)) for m in range(1, 5)]

    kv = jnp.concatenate([soft_key, soft_value], axis=1)
    far_kv = [send(kv, window(m, rooms)) for m in range(1, SPAN + 1)]

    intra = pl.pallas_call(
        intra_kernel, grid=(H,),
        in_specs=[smem, smem, per_head(), per_head(), per_head(), whole(T, H), whole(H, T)],
        out_specs=per_head(), out_shape=shape(T, width),
        scratch_shapes=[pltpu.VMEM((T, T), F32)], name="intra",
    )(starts, lengths, lin_query, lin_key, lin_value, cum, cum_t)

    near, near_low, across = pl.pallas_call(
        combine_kernel,
        out_shape=[shape(width, D), shape(width, D, kind=BF16), shape(H, D)], name="combine",
    )(*states)
    second = [(i, j) for i, j in window(4, rooms) if i % SPAN != 0]
    far_state = send(near_low, second)

    heads, squares = pl.pallas_call(
        carry_kernel, grid=(H,),
        in_specs=[smem, smem, per_head(), per_head(),
                  pl.BlockSpec((D, D), lambda h: (h, 0)), pl.BlockSpec((D, D), lambda h: (h, 0)),
                  whole(H, D), whole(T, H)],
        out_specs=[per_head(), whole(8, T)],
        out_shape=[shape(T, width), shape(8, T)],
        scratch_shapes=[pltpu.VMEM((T, D), F32)], name="carry",
    )(starts, lengths, lin_query, intra, near, far_state, across, cum)
    step = 1
    while step < share:
        squares = squares + lax.ppermute(squares, "head", [(i, i ^ step) for i in range(share)])
        step *= 2

    soft_out = pl.pallas_call(
        soft_kernel, grid=(H,),
        in_specs=[smem, smem, per_head()] + [whole(T, 2 * D)] * (SPAN + 1),
        out_specs=per_head(), out_shape=shape(T, width, kind=BF16),
        scratch_shapes=[pltpu.VMEM((SPAN + 1, T, D), BF16), pltpu.VMEM((SPAN + 1, T, 2 * D), BF16),
                        pltpu.VMEM((T, T), F32), pltpu.VMEM((SPAN + 1, T, T), F32),
                        pltpu.VMEM((T, D), F32), pltpu.VMEM((T, 2 * D), F32)], name="soft",
    )(starts, lengths, soft_query, kv, *far_kv)

    lin_out = pl.pallas_call(
        functools.partial(norm_kernel, features=width * share), grid=(H,),
        in_specs=[per_head(), per_head(), per_head(1), whole(8, T)],
        out_specs=per_head(), out_shape=shape(T, width, kind=BF16),
        scratch_shapes=[pltpu.VMEM((T, D), F32)], name="norm",
    )(heads, lin_gate, norm_gain.reshape(1, width), squares)
    return (lin_out, soft_out)


def solution(mesh):
    wide = P("ctx", "head")
    return jax.shard_map(
        per_device, mesh=mesh,
        in_specs=(wide, wide, wide, wide, wide, P("head"), wide, wide, wide, P(), P()),
        out_specs=(wide, wide), check_vma=False,
    )
```

```python
import functools
import jax
import jax.numpy as jnp
from jax import lax
from jax.experimental import pallas as pl
from jax.experimental.pallas import tpu as pltpu
from jax.sharding import PartitionSpec as P


T = 384
D = 128
H = 8
SPAN = 8
NEG = -1e30
EPS = 1e-06
GONE = -1e5
ROW = 4
PAIR = H // ROW
EXTRA = 16
HI = lax.Precision.HIGHEST
F32 = jnp.float32
BF16 = jnp.bfloat16
NT = (((1,), (1,)), ((), ()))
TN = (((0,), (0,)), ((), ()))


def iota(shape, axis):
    return lax.broadcasted_iota(jnp.int32, shape, axis)


def marks(starts, lengths):
    device = lax.axis_index("ctx")
    room = device // SPAN
    place = device % SPAN
    first = device * T
    at_start = place == 0
    bound = jnp.where(at_start, starts[room] - first, 0)
    earlier = jnp.maximum(room - 1, 0)
    end_prev = jnp.where(at_start & (room > 0), starts[earlier] + lengths[earlier] - first, 0)
    end_cur = starts[room] + lengths[room] - first
    return room, place, bound, end_prev, end_cur


def valid_rows(shape, bound, end_prev, end_cur):
    rows = iota(shape, 0)
    return rows < jnp.where(rows < bound, end_prev, end_cur)


def state_kernel(starts, lengths, key, value, dec_t, s0, s1, s2, s3, cum, cum_t, pack, rest):
    room, place, bound, end_prev, end_cur = marks(starts, lengths)
    lower = (iota((T, T), 1) <= iota((T, T), 0)).astype(F32)
    dec = dec_t[...]
    col = lax.dot_general(lower, dec, NT, precision=HI, preferred_element_type=F32)
    cum[...] = col
    cum_t[...] = lax.dot_general(dec, lower, NT, precision=HI, preferred_element_type=F32)
    rows = iota((T, 1), 0)
    keep = (rows >= bound) & (rows < end_cur)
    last = col[T - 1:T, :]
    to_end = jnp.where(keep, jnp.exp(last - col), 0.0)
    total = jnp.where(place == 0, GONE, last)
    for h in range(H):
        part = slice(h * D, (h + 1) * D)
        scaled = (key[:, part].astype(F32) * to_end[:, h:h + 1]).astype(BF16)
        state = lax.dot_general(scaled, value[:, part], TN, preferred_element_type=F32)
        pack[h // PAIR, (h % PAIR) * D:(h % PAIR + 1) * D, :] = state.astype(BF16)
    at = iota((EXTRA, D), 0)
    for w in range(ROW):
        table = jnp.zeros((EXTRA, D), F32)
        for j in range(PAIR):
            one = jnp.broadcast_to(total[:, w * PAIR + j:w * PAIR + j + 1], (EXTRA, D))
            a = one.astype(BF16).astype(F32)
            b = (one - a).astype(BF16).astype(F32)
            c = one - a - b
            for i, x in enumerate((a, b, c)):
                table = jnp.where(at == 3 * j + i, x, table)
        rest[w] = table.astype(BF16)
    x = place % ROW
    for step, out in enumerate((s0, s1, s2, s3)):
        w = (x + step) % ROW
        out[0:PAIR * D, :] = pack[w]
        out[PAIR * D:PAIR * D + EXTRA, :] = rest[w]


def log_decays(ref):
    table = ref[PAIR * D:PAIR * D + EXTRA, :].astype(F32)
    return [table[3 * j:3 * j + 1] + table[3 * j + 1:3 * j + 2] + table[3 * j + 2:3 * j + 3]
            for j in range(PAIR)]


def gather_row(own, r1, r2, r3, states, logs):
    x = (lax.axis_index("ctx") % SPAN) % ROW
    for step, ref in enumerate((own, r1, r2, r3)):
        w = (x - step + ROW) % ROW
        states[w] = ref[0:PAIR * D, :].astype(F32)
        for j, one in enumerate(log_decays(ref)):
            logs[w, 8 * j:8 * j + 8, :] = jnp.broadcast_to(one, (8, D))


def row_kernel(own, r1, r2, r3, out, states, logs):
    gather_row(own, r1, r2, r3, states, logs)
    at = iota((EXTRA, D), 0)
    table = jnp.zeros((EXTRA, D), F32)
    for j in range(PAIR):
        part = slice(j * D, (j + 1) * D)
        c = [logs[w, 8 * j:8 * j + 1, :] for w in range(ROW)]
        total = (states[3, part, :] + jnp.exp(c[3]) * states[2, part, :]
                 + jnp.exp(c[3] + c[2]) * states[1, part, :]
                 + jnp.exp(c[3] + c[2] + c[1]) * states[0, part, :])
        out[part, :] = total.astype(BF16)
        one = jnp.broadcast_to(c[0] + c[1] + c[2] + c[3], (EXTRA, D))
        a = one.astype(BF16).astype(F32)
        b = (one - a).astype(BF16).astype(F32)
        for i, x in enumerate((a, b, one - a - b)):
            table = jnp.where(at == 3 * j + i, x, table)
    out[PAIR * D:PAIR * D + EXTRA, :] = table.astype(BF16)


def prefix_kernel(own, r1, r2, r3, z1, z2, p0, p1, p2, p3, states, logs, ready):
    gather_row(own, r1, r2, r3, states, logs)
    decay = log_decays(z1)
    for j in range(PAIR):
        part = slice(j * D, (j + 1) * D)
        c = [logs[w, 8 * j:8 * j + 1, :] for w in range(ROW)]
        state = (z1[part, :].astype(F32) + jnp.exp(decay[j]) * z2[part, :].astype(F32))
        ready[0, part, :] = state.astype(BF16)
        state1 = states[0, part, :]
        ready[1, part, :] = (state1 + jnp.exp(c[0]) * state).astype(BF16)
        state2 = states[1, part, :] + jnp.exp(c[1]) * state1
        ready[2, part, :] = (state2 + jnp.exp(c[0] + c[1]) * state).astype(BF16)
        state3 = states[2, part, :] + jnp.exp(c[2]) * state2
        ready[3, part, :] = (state3 + jnp.exp(c[0] + c[1] + c[2]) * state).astype(BF16)
    x = (lax.axis_index("ctx") % SPAN) % ROW
    for step, out in enumerate((p0, p1, p2, p3)):
        out[...] = ready[(x + step) % ROW]


def intra_kernel(starts, lengths, query, key, value, cum, cum_t, out, bias):
    room, place, bound, end_prev, end_cur = marks(starts, lengths)
    t = iota((T, T), 0)
    i = iota((T, T), 1)
    seen = (i <= t) & ((i >= bound) | (t < bound))
    bias[...] = jnp.where(seen, 0.0, NEG)
    for h in range(H):
        lanes = slice(h * D, (h + 1) * D)
        for r in range(T // D):
            part = slice(r * D, (r + 1) * D)
            wide = (r + 1) * D
            scores = lax.dot_general(query[part, lanes], key[0:wide, lanes], NT,
                                     preferred_element_type=F32)
            gap = (cum[part, h:h + 1] - cum_t[h:h + 1, 0:wide]) + bias[part, 0:wide]
            weights = (scores * jnp.exp(gap)).astype(BF16)
            out[part, lanes] = jnp.dot(weights, value[0:wide, lanes], preferred_element_type=F32)


def carry_kernel(starts, lengths, query, intra, p0, p1, p2, p3, cum, out, squares, states):
    room, place, bound, end_prev, end_cur = marks(starts, lengths)
    x = place % ROW
    for step, ref in enumerate((p0, p1, p2, p3)):
        states[(x - step + ROW) % ROW] = ref[...]
    rows = iota((T, 1), 0)
    valid = rows < jnp.where(rows < bound, end_prev, end_cur)
    enters = (rows < jnp.where(place > 0, T, bound)) & valid
    enter = jnp.where(enters, jnp.exp(cum[...]), 0.0)
    live = jnp.where(valid, 1.0, 0.0)
    acc = jnp.zeros((T, D), F32)
    for h in range(H):
        lanes = slice(h * D, (h + 1) * D)
        state = states[h // PAIR, (h % PAIR) * D:(h % PAIR + 1) * D, :]
        carried = jnp.dot(query[:, lanes], state, preferred_element_type=F32)
        heads = intra[:, lanes] * live + enter[:, h:h + 1] * carried
        out[:, lanes] = heads
        acc += heads * heads
    squares[...] = lax.dot_general(jnp.ones((8, D), F32), acc, NT, precision=HI,
                                   preferred_element_type=F32)


def norm_kernel(heads, gate, gain, squares, others, out, *, features):
    pick = (iota((8, D), 0) == 0).astype(F32)
    sums = lax.dot_general(squares[...] + others[...], pick, TN, precision=HI,
                           preferred_element_type=F32)
    scale = lax.rsqrt(sums * (1.0 / features) + EPS)
    for h in range(heads.shape[1] // D):
        lanes = slice(h * D, (h + 1) * D)
        gated = jax.nn.sigmoid(gate[:, lanes].astype(F32))
        out[:, lanes] = (heads[:, lanes] * scale * gain[:, lanes] * gated).astype(BF16)


def soft_kernel(starts, lengths, query, own, f1, f2, f3, f4, f5, f6, f7, f8, out,
                keys, values, top, acc):
    room, place, bound, end_prev, end_cur = marks(starts, lengths)
    tail = place == 0
    count = jnp.where(tail, jnp.where(room > 0, SPAN, 0), place)
    begin_room = jnp.where(tail, jnp.maximum(room - 1, 0), room)
    begin = starts[begin_room] - begin_room * SPAN * T
    factor = (D ** -0.5) * 1.4426950408889634
    ones = jnp.ones((T, D), BF16)
    for m, ref in enumerate((own, f1, f2, f3, f4, f5, f6, f7, f8)):
        @pl.when(m <= count)
        def _():
            keys[m] = ref[:, 0:D]
            values[m, :, 0:D] = ref[:, D:2 * D]
            values[m, :, D:2 * D] = ones

    def attend(m, size, hidden, fresh=False):
        k = keys[m]
        v = values[m]
        for h in range(H):
            x = lax.dot_general(query[0:size, h * D:(h + 1) * D], k, NT,
                                preferred_element_type=F32)
            if hidden is not None:
                x = x + hidden
            parts = [x[:, j * D:(j + 1) * D] for j in range(T // D)]
            best = functools.reduce(jnp.maximum, parts)
            peak = jnp.broadcast_to(jnp.max(best, axis=1, keepdims=True), (size, D)) * factor
            if not fresh:
                old = top[h, 0:size, :]
                peak = jnp.maximum(old, peak)
                shrink = jnp.exp2(old - peak)
            top[h, 0:size, :] = peak
            p = jnp.concatenate([jnp.exp2(y * factor - peak).astype(BF16) for y in parts], axis=1)
            mixed = jnp.dot(p, v, preferred_element_type=F32)
            if not fresh:
                mixed = mixed + acc[h, 0:size, :] * jnp.concatenate([shrink, shrink], axis=1)
            acc[h, 0:size, :] = mixed

    t = iota((T, T), 0)
    i = iota((T, T), 1)
    seen = (i <= t) & ((i >= bound) | (t < bound))
    attend(0, T, jnp.where(seen, 0.0, NEG), fresh=True)

    @pl.when(place > 0)
    def _():
        def middle(m, _):
            attend(m, T, None)
            return 0

        lax.fori_loop(1, count, middle, 0)
        attend(count, T, jnp.where(iota((1, T), 1) < begin, NEG, 0.0))

    half = T // 2

    @pl.when(tail & (count > 0))
    def _():
        def one(m, _):
            row_ok = iota((half, T), 0) < bound
            first_key = jnp.where(m == count, begin, 0)
            attend(m, half, jnp.where(row_ok & (iota((half, T), 1) >= first_key), 0.0, NEG))
            return 0

        lax.fori_loop(1, count + 1, one, 0)

    valid = valid_rows((T, 1), bound, end_prev, end_cur)
    for h in range(H):
        mixed = acc[h, :, 0:D] / acc[h, :, D:2 * D]
        out[:, h * D:(h + 1) * D] = jnp.where(valid, mixed, 0.0).astype(BF16)


smem = pl.BlockSpec(memory_space=pltpu.SMEM)
vmem = pl.BlockSpec(memory_space=pltpu.VMEM)


def shape(*dims, kind=F32):
    return jax.ShapeDtypeStruct(dims, kind)


def call(kernel, tables, operands, outs, scratch=()):
    return pl.pallas_call(
        kernel, in_specs=[smem] * tables + [vmem] * (len(operands) - tables),
        out_specs=[vmem] * len(outs), out_shape=list(outs), scratch_shapes=list(scratch),
    )(*operands)


def window(distance, rooms):
    pairs = []
    for room in range(rooms):
        base = room * SPAN
        for i in range(base, base + SPAN):
            j = i + distance
            if j <= base + SPAN and j < rooms * SPAN:
                pairs.append((i, j))
    return pairs


def per_device(lin_query, lin_key, lin_value, lin_gate, lin_decay, norm_gain,
               soft_query, soft_key, soft_value, starts, lengths):
    places = lax.axis_size("ctx")
    rooms = places // SPAN
    share = lax.axis_size("head")
    width = H * D
    piece = PAIR * D
    around = [[(i, i - i % ROW + (i + step) % ROW) for i in range(places)] for step in range(ROW)]
    onward = [(i, i + ROW) for i in range(places - ROW)]
    beyond = [(i, i + 2 * ROW) for i in range(places - 2 * ROW) if i // ROW % 2 == 0]
    send = lambda x, pairs: lax.ppermute(x, "ctx", pairs)
    packed = shape(piece + EXTRA, D, kind=BF16)

    *slices, cum, cum_t = call(
        state_kernel, 2, (starts, lengths, lin_key, lin_value, lin_decay.T),
        [packed] * ROW + [shape(T, H), shape(H, T)],
        [pltpu.VMEM((ROW, piece, D), BF16), pltpu.VMEM((ROW, EXTRA, D), BF16)])
    row = [slices[0]] + [send(slices[j], around[j]) for j in range(1, ROW)]

    kv = jnp.concatenate([soft_key, soft_value], axis=1)
    far_kv = [send(kv, window(m, rooms)) for m in range(1, SPAN + 1)]

    intra, = call(intra_kernel, 2,
                  (starts, lengths, lin_query, lin_key, lin_value, cum, cum_t),
                  [shape(T, width)], [pltpu.VMEM((T, T), F32)])

    table = [pltpu.VMEM((ROW, piece, D), F32), pltpu.VMEM((ROW, 8 * PAIR, D), F32)]
    row_total, = call(row_kernel, 0, row, [packed], table)
    above = send(row_total, onward)
    above2 = send(row_total, beyond)
    ready = call(prefix_kernel, 0, (*row, above, above2),
                 [shape(piece, D, kind=BF16)] * ROW,
                 table + [pltpu.VMEM((ROW, piece, D), BF16)])
    before = [ready[0]] + [send(ready[j], around[j]) for j in range(1, ROW)]

    heads, squares = call(
        carry_kernel, 2, (starts, lengths, lin_query, intra, *before, cum),
        [shape(T, width), shape(8, T)], [pltpu.VMEM((ROW, piece, D), BF16)])
    step = 1
    others = jnp.zeros_like(squares)
    while step < share:
        if step > 1:
            squares = squares + others
        others = lax.ppermute(squares, "head", [(i, i ^ step) for i in range(share)])
        step *= 2

    soft_out, = call(
        soft_kernel, 2, (starts, lengths, soft_query, kv, *far_kv),
        [shape(T, width, kind=BF16)],
        [pltpu.VMEM((SPAN + 1, T, D), BF16), pltpu.VMEM((SPAN + 1, T, 2 * D), BF16),
         pltpu.VMEM((H, T, D), F32), pltpu.VMEM((H, T, 2 * D), F32)])

    lin_out, = call(
        functools.partial(norm_kernel, features=width * share), 0,
        (heads, lin_gate, norm_gain.reshape(1, width), squares, others),
        [shape(T, width, kind=BF16)])
    return (lin_out, soft_out)


def solution(mesh):
    wide = P("ctx", "head")
    return jax.shard_map(
        per_device, mesh=mesh,
        in_specs=(wide, wide, wide, wide, wide, P("head"), wide, wide, wide, P(), P()),
        out_specs=(wide, wide), check_vma=False,
    )
```

```python
import functools
import jax
import jax.numpy as jnp
from jax import lax
from jax.experimental import pallas as pl
from jax.experimental.pallas import tpu as pltpu
from jax.sharding import PartitionSpec as P


T = 384
D = 128
H = 8
SPAN = 8
NEG = -1e30
GROUP = 2
EPS = 1e-06
GONE = -1e5
ROW = 4
PAIR = H // ROW
EXTRA = 16
HI = lax.Precision.HIGHEST
F32 = jnp.float32
BF16 = jnp.bfloat16
NT = (((1,), (1,)), ((), ()))
TN = (((0,), (0,)), ((), ()))


def iota(shape, axis):
    return lax.broadcasted_iota(jnp.int32, shape, axis)


def marks(starts, lengths):
    device = lax.axis_index("ctx")
    room = device // SPAN
    place = device % SPAN
    first = device * T
    at_start = place == 0
    bound = jnp.where(at_start, starts[room] - first, 0)
    earlier = jnp.maximum(room - 1, 0)
    end_prev = jnp.where(at_start & (room > 0), starts[earlier] + lengths[earlier] - first, 0)
    end_cur = starts[room] + lengths[room] - first
    return room, place, bound, end_prev, end_cur


def valid_rows(shape, bound, end_prev, end_cur):
    rows = iota(shape, 0)
    return rows < jnp.where(rows < bound, end_prev, end_cur)


def state_kernel(starts, lengths, key, value, dec_t, soft_key, soft_value, s0, s1, s2, s3, cum,
                 cum_t, both, pack, rest):
    both[:, 0:D] = soft_key[...]
    both[:, D:2 * D] = soft_value[...]
    _, place, bound, _, end_cur = marks(starts, lengths)
    lower = (iota((T, T), 1) <= iota((T, T), 0)).astype(F32)
    dec = dec_t[...]
    col = lax.dot_general(lower, dec, NT, precision=HI, preferred_element_type=F32)
    cum[...] = col
    cum_t[...] = lax.dot_general(dec, lower, NT, precision=HI, preferred_element_type=F32)
    rows = iota((T, 1), 0)
    keep = (rows >= bound) & (rows < end_cur)
    last = col[T - 1:T, :]
    to_end = jnp.where(keep, jnp.exp(last - col), 0.0)
    total = jnp.where(place == 0, GONE, last)
    for h in range(H):
        part = slice(h * D, (h + 1) * D)
        scaled = (key[:, part].astype(F32) * to_end[:, h:h + 1]).astype(BF16)
        state = lax.dot_general(scaled, value[:, part], TN, preferred_element_type=F32)
        pack[h // PAIR, (h % PAIR) * D:(h % PAIR + 1) * D, :] = state.astype(BF16)
    at = iota((EXTRA, D), 0)
    for w in range(ROW):
        table = jnp.zeros((EXTRA, D), F32)
        for j in range(PAIR):
            one = jnp.broadcast_to(total[:, w * PAIR + j:w * PAIR + j + 1], (EXTRA, D))
            a = one.astype(BF16).astype(F32)
            b = (one - a).astype(BF16).astype(F32)
            c = one - a - b
            for i, x in enumerate((a, b, c)):
                table = jnp.where(at == 3 * j + i, x, table)
        rest[w] = table.astype(BF16)
    x = place % ROW
    for step, out in enumerate((s0, s1, s2, s3)):
        w = (x + step) % ROW
        out[0:PAIR * D, :] = pack[w]
        out[PAIR * D:PAIR * D + EXTRA, :] = rest[w]


def log_decays(ref):
    table = ref[PAIR * D:PAIR * D + EXTRA, :].astype(F32)
    return [table[3 * j:3 * j + 1] + table[3 * j + 1:3 * j + 2] + table[3 * j + 2:3 * j + 3]
            for j in range(PAIR)]


def gather_row(own, r1, r2, r3, states, logs):
    x = (lax.axis_index("ctx") % SPAN) % ROW
    for step, ref in enumerate((own, r1, r2, r3)):
        w = (x - step + ROW) % ROW
        states[w] = ref[0:PAIR * D, :].astype(F32)
        for j, one in enumerate(log_decays(ref)):
            logs[w, 8 * j:8 * j + 8, :] = jnp.broadcast_to(one, (8, D))


def row_kernel(own, r1, r2, r3, out, states, logs):
    gather_row(own, r1, r2, r3, states, logs)
    at = iota((EXTRA, D), 0)
    table = jnp.zeros((EXTRA, D), F32)
    for j in range(PAIR):
        part = slice(j * D, (j + 1) * D)
        c = [logs[w, 8 * j:8 * j + 1, :] for w in range(ROW)]
        total = (states[3, part, :] + jnp.exp(c[3]) * states[2, part, :]
                 + jnp.exp(c[3] + c[2]) * states[1, part, :]
                 + jnp.exp(c[3] + c[2] + c[1]) * states[0, part, :])
        out[part, :] = total.astype(BF16)
        one = jnp.broadcast_to(c[0] + c[1] + c[2] + c[3], (EXTRA, D))
        a = one.astype(BF16).astype(F32)
        b = (one - a).astype(BF16).astype(F32)
        for i, x in enumerate((a, b, one - a - b)):
            table = jnp.where(at == 3 * j + i, x, table)
    out[PAIR * D:PAIR * D + EXTRA, :] = table.astype(BF16)


def prefix_kernel(own, r1, r2, r3, z1, z2, p0, p1, p2, p3, states, logs, ready):
    gather_row(own, r1, r2, r3, states, logs)
    decay = log_decays(z1)
    for j in range(PAIR):
        part = slice(j * D, (j + 1) * D)
        c = [logs[w, 8 * j:8 * j + 1, :] for w in range(ROW)]
        state = (z1[part, :].astype(F32) + jnp.exp(decay[j]) * z2[part, :].astype(F32))
        ready[0, part, :] = state.astype(BF16)
        state1 = states[0, part, :]
        ready[1, part, :] = (state1 + jnp.exp(c[0]) * state).astype(BF16)
        state2 = states[1, part, :] + jnp.exp(c[1]) * state1
        ready[2, part, :] = (state2 + jnp.exp(c[0] + c[1]) * state).astype(BF16)
        state3 = states[2, part, :] + jnp.exp(c[2]) * state2
        ready[3, part, :] = (state3 + jnp.exp(c[0] + c[1] + c[2]) * state).astype(BF16)
    x = (lax.axis_index("ctx") % SPAN) % ROW
    for step, out in enumerate((p0, p1, p2, p3)):
        out[...] = ready[(x + step) % ROW]


def intra_kernel(starts, lengths, query, key, value, cum, cum_t, out, bias):
    _, _, bound, _, _ = marks(starts, lengths)
    t = iota((T, T), 0)
    i = iota((T, T), 1)
    seen = (i <= t) & ((i >= bound) | (t < bound))
    bias[...] = jnp.where(seen, 0.0, NEG)
    for h in range(H):
        lanes = slice(h * D, (h + 1) * D)
        for r in range(T // D):
            part = slice(r * D, (r + 1) * D)
            wide = (r + 1) * D
            scores = lax.dot_general(query[part, lanes], key[0:wide, lanes], NT,
                                     preferred_element_type=F32)
            gap = (cum[part, h:h + 1] - cum_t[h:h + 1, 0:wide]) + bias[part, 0:wide]
            weights = (scores * jnp.exp(gap)).astype(BF16)
            out[part, lanes] = jnp.dot(weights, value[0:wide, lanes], preferred_element_type=F32)


def carry_kernel(starts, lengths, query, intra, p0, p1, p2, p3, cum, out, squares, states):
    _, place, bound, end_prev, end_cur = marks(starts, lengths)
    x = place % ROW
    for step, ref in enumerate((p0, p1, p2, p3)):
        states[(x - step + ROW) % ROW] = ref[...]
    rows = iota((T, 1), 0)
    valid = rows < jnp.where(rows < bound, end_prev, end_cur)
    enters = (rows < jnp.where(place > 0, T, bound)) & valid
    enter = jnp.where(enters, jnp.exp(cum[...]), 0.0)
    live = jnp.where(valid, 1.0, 0.0)
    acc = jnp.zeros((T, D), F32)
    for h in range(H):
        lanes = slice(h * D, (h + 1) * D)
        state = states[h // PAIR, (h % PAIR) * D:(h % PAIR + 1) * D, :]
        carried = jnp.dot(query[:, lanes], state, preferred_element_type=F32)
        heads = intra[:, lanes] * live + enter[:, h:h + 1] * carried
        out[:, lanes] = heads
        acc += heads * heads
    squares[...] = lax.dot_general(jnp.ones((8, D), F32), acc, NT, precision=HI,
                                   preferred_element_type=F32)


def norm_kernel(heads, gate, gain, squares, others, out, *, features):
    pick = (iota((8, D), 0) == 0).astype(F32)
    sums = lax.dot_general(squares[...] + others[...], pick, TN, precision=HI,
                           preferred_element_type=F32)
    scale = lax.rsqrt(sums * (1.0 / features) + EPS)
    for h in range(heads.shape[1] // D):
        lanes = slice(h * D, (h + 1) * D)
        gated = jax.nn.sigmoid(gate[:, lanes].astype(F32))
        out[:, lanes] = (heads[:, lanes] * scale * gain[:, lanes] * gated).astype(BF16)


def soft_kernel(starts, lengths, query, own, f1, f2, f3, f4, f5, f6, f7, f8, out,
                keys, values, asks, top, acc):
    room, place, bound, end_prev, end_cur = marks(starts, lengths)
    tail = place == 0
    count = jnp.where(tail, jnp.where(room > 0, SPAN, 0), place)
    begin_room = jnp.where(tail, jnp.maximum(room - 1, 0), room)
    begin = starts[begin_room] - begin_room * SPAN * T
    factor = (D ** -0.5) * 1.4426950408889634
    ones = jnp.ones((T, D), BF16)
    for m, ref in enumerate((own, f1, f2, f3, f4, f5, f6, f7, f8)):
        @pl.when(m <= count)
        def _():
            keys[m] = ref[:, 0:D]
            values[m, :, 0:D] = ref[:, D:2 * D]
            values[m, :, D:2 * D] = ones

    for h in range(H):
        asks[h] = query[:, h * D:(h + 1) * D]

    def attend(m, size, hidden, fresh=False):
        k = keys[m]
        v = values[m]
        span = GROUP if size == T else 1
        many = span * size

        def ask(h):
            return lax.dot_general(asks[h:h + span, 0:size, :].reshape(many, D), k, NT,
                                   preferred_element_type=F32)

        heads = range(0, H, span)
        ahead = ask(0)
        for h in heads:
            x = ahead
            if h + span < H:
                ahead = ask(h + span)
            if hidden is not None:
                x = (x.reshape(span, size, T) + hidden[None]).reshape(many, T)
            parts = [x[:, j * D:(j + 1) * D] for j in range(T // D)]
            best = functools.reduce(jnp.maximum, parts)
            peak = jnp.broadcast_to(jnp.max(best, axis=1, keepdims=True), (many, D)) * factor
            if not fresh:
                old = top[h:h + span, 0:size, :].reshape(many, D)
                peak = jnp.maximum(old, peak)
                shrink = jnp.exp2(old - peak)
            top[h:h + span, 0:size, :] = peak.reshape(span, size, D)
            p = jnp.concatenate([jnp.exp2(y * factor - peak).astype(BF16) for y in parts], axis=1)
            mixed = jnp.dot(p, v, preferred_element_type=F32)
            if not fresh:
                kept = acc[h:h + span, 0:size, :].reshape(many, 2 * D)
                mixed = mixed + kept * jnp.concatenate([shrink, shrink], axis=1)
            acc[h:h + span, 0:size, :] = mixed.reshape(span, size, 2 * D)

    t = iota((T, T), 0)
    i = iota((T, T), 1)
    seen = (i <= t) & ((i >= bound) | (t < bound))
    attend(0, T, jnp.where(seen, 0.0, NEG), fresh=True)

    @pl.when(place > 0)
    def _():
        def middle(m, _):
            attend(m, T, None)
            return 0

        lax.fori_loop(1, count, middle, 0)
        attend(count, T, jnp.where(iota((1, T), 1) < begin, NEG, 0.0))

    half = T // 2

    @pl.when(tail & (count > 0))
    def _():
        def one(m, _):
            row_ok = iota((half, T), 0) < bound
            first_key = jnp.where(m == count, begin, 0)
            attend(m, half, jnp.where(row_ok & (iota((half, T), 1) >= first_key), 0.0, NEG))
            return 0

        lax.fori_loop(1, count + 1, one, 0)

    valid = valid_rows((T, 1), bound, end_prev, end_cur)
    for h in range(H):
        mixed = acc[h, :, 0:D] / acc[h, :, D:2 * D]
        out[:, h * D:(h + 1) * D] = jnp.where(valid, mixed, 0.0).astype(BF16)


smem = pl.BlockSpec(memory_space=pltpu.SMEM)
vmem = pl.BlockSpec(memory_space=pltpu.VMEM)


def shape(*dims, kind=F32):
    return jax.ShapeDtypeStruct(dims, kind)


def call(kernel, tables, operands, outs, scratch=()):
    return pl.pallas_call(
        kernel, in_specs=[smem] * tables + [vmem] * (len(operands) - tables),
        out_specs=[vmem] * len(outs), out_shape=list(outs), scratch_shapes=list(scratch),
    )(*operands)


def window(distance, rooms):
    pairs = []
    for room in range(rooms):
        base = room * SPAN
        for i in range(base, base + SPAN):
            j = i + distance
            if j <= base + SPAN and j < rooms * SPAN:
                pairs.append((i, j))
    return pairs


def per_device(lin_query, lin_key, lin_value, lin_gate, lin_decay, norm_gain,
               soft_query, soft_key, soft_value, starts, lengths):
    places = lax.axis_size("ctx")
    rooms = places // SPAN
    share = lax.axis_size("head")
    width = H * D
    piece = PAIR * D
    around = [[(i, i - i % ROW + (i + step) % ROW) for i in range(places)] for step in range(ROW)]
    onward = [(i, i + ROW) for i in range(places - ROW)]
    beyond = [(i, i + 2 * ROW) for i in range(places - 2 * ROW) if i // ROW % 2 == 0]

    def send(x, pairs):
        return lax.ppermute(x, "ctx", pairs)

    packed = shape(piece + EXTRA, D, kind=BF16)

    pair = shape(T, 2 * D, kind=BF16)
    *slices, cum, cum_t, kv = call(
        state_kernel, 2,
        (starts, lengths, lin_key, lin_value, lin_decay.T, soft_key, soft_value),
        [packed] * ROW + [shape(T, H), shape(H, T), pair],
        [pltpu.VMEM((ROW, piece, D), BF16), pltpu.VMEM((ROW, EXTRA, D), BF16)])
    row = [slices[0]] + [send(slices[j], around[j]) for j in range(1, ROW)]

    intra, = call(intra_kernel, 2,
                  (starts, lengths, lin_query, lin_key, lin_value, cum, cum_t),
                  [shape(T, width)], [pltpu.VMEM((T, T), F32)])

    table = [pltpu.VMEM((ROW, piece, D), F32), pltpu.VMEM((ROW, 8 * PAIR, D), F32)]
    row_total, = call(row_kernel, 0, row, [packed], table)
    above = send(row_total, onward)
    above2 = send(row_total, beyond)
    ready = call(
        prefix_kernel, 0, (*row, above, above2), [shape(piece, D, kind=BF16)] * ROW,
        table + [pltpu.VMEM((ROW, piece, D), BF16)])
    before = [ready[0]] + [send(ready[j], around[j]) for j in range(1, ROW)]

    far_kv = [send(kv, window(m, rooms)) for m in range(1, SPAN + 1)]

    heads, squares = call(
        carry_kernel, 2, (starts, lengths, lin_query, intra, *before, cum),
        [shape(T, width), shape(8, T)], [pltpu.VMEM((ROW, piece, D), BF16)])
    step = 1
    others = jnp.zeros_like(squares)
    while step < share:
        if step > 1:
            squares = squares + others
        others = lax.ppermute(squares, "head", [(i, i ^ step) for i in range(share)])
        step *= 2

    soft_out, = call(
        soft_kernel, 2, (starts, lengths, soft_query, kv, *far_kv),
        [shape(T, width, kind=BF16)],
        [pltpu.VMEM((SPAN + 1, T, D), BF16), pltpu.VMEM((SPAN + 1, T, 2 * D), BF16),
         pltpu.VMEM((H, T, D), BF16), pltpu.VMEM((H, T, D), F32),
         pltpu.VMEM((H, T, 2 * D), F32)])

    lin_out, = call(
        functools.partial(norm_kernel, features=width * share), 0,
        (heads, lin_gate, norm_gain.reshape(1, width), squares, others),
        [shape(T, width, kind=BF16)])
    return (lin_out, soft_out)


def solution(mesh):
    wide = P("ctx", "head")
    return jax.shard_map(
        per_device, mesh=mesh,
        in_specs=(wide, wide, wide, wide, wide, P("head"), wide, wide, wide, P(), P()),
        out_specs=(wide, wide), check_vma=False,
    )
```

```python
import functools
import jax
import jax.numpy as jnp
from jax import lax
from jax.experimental import pallas as pl
from jax.experimental.pallas import tpu as pltpu
from jax.sharding import PartitionSpec as P


T = 384
D = 128
H = 8
SPAN = 8
NEG = -1e30
PART = 4
GROUP = 2
EPS = 1e-06
GONE = -1e5
ROW = 4
PAIR = H // ROW
EXTRA = 16
HI = lax.Precision.HIGHEST
F32 = jnp.float32
BF16 = jnp.bfloat16
NT = (((1,), (1,)), ((), ()))
TN = (((0,), (0,)), ((), ()))


def iota(shape, axis):
    return lax.broadcasted_iota(jnp.int32, shape, axis)


def marks(starts, lengths):
    device = lax.axis_index("ctx")
    room = device // SPAN
    place = device % SPAN
    first = device * T
    at_start = place == 0
    bound = jnp.where(at_start, starts[room] - first, 0)
    earlier = jnp.maximum(room - 1, 0)
    end_prev = jnp.where(at_start & (room > 0), starts[earlier] + lengths[earlier] - first, 0)
    end_cur = starts[room] + lengths[room] - first
    return room, place, bound, end_prev, end_cur


def valid_rows(shape, bound, end_prev, end_cur):
    rows = iota(shape, 0)
    return rows < jnp.where(rows < bound, end_prev, end_cur)


def state_kernel(starts, lengths, key, value, dec_t, soft_key, soft_value, s0, s1, s2, s3, cum,
                 cum_t, both, pack, rest):
    both[:, 0:D] = soft_key[...]
    both[:, D:2 * D] = soft_value[...]
    _, place, bound, _, end_cur = marks(starts, lengths)
    lower = (iota((T, T), 1) <= iota((T, T), 0)).astype(F32)
    dec = dec_t[...]
    col = lax.dot_general(lower, dec, NT, precision=HI, preferred_element_type=F32)
    cum[...] = col
    cum_t[...] = lax.dot_general(dec, lower, NT, precision=HI, preferred_element_type=F32)
    rows = iota((T, 1), 0)
    keep = (rows >= bound) & (rows < end_cur)
    last = col[T - 1:T, :]
    to_end = jnp.where(keep, jnp.exp(last - col), 0.0)
    total = jnp.where(place == 0, GONE, last)
    for h in range(H):
        part = slice(h * D, (h + 1) * D)
        scaled = (key[:, part].astype(F32) * to_end[:, h:h + 1]).astype(BF16)
        state = lax.dot_general(scaled, value[:, part], TN, preferred_element_type=F32)
        pack[h // PAIR, (h % PAIR) * D:(h % PAIR + 1) * D, :] = state.astype(BF16)
    at = iota((EXTRA, D), 0)
    for w in range(ROW):
        table = jnp.zeros((EXTRA, D), F32)
        for j in range(PAIR):
            one = jnp.broadcast_to(total[:, w * PAIR + j:w * PAIR + j + 1], (EXTRA, D))
            a = one.astype(BF16).astype(F32)
            b = (one - a).astype(BF16).astype(F32)
            c = one - a - b
            for i, x in enumerate((a, b, c)):
                table = jnp.where(at == 3 * j + i, x, table)
        rest[w] = table.astype(BF16)
    x = place % ROW
    for step, out in enumerate((s0, s1, s2, s3)):
        w = (x + step) % ROW
        out[0:PAIR * D, :] = pack[w]
        out[PAIR * D:PAIR * D + EXTRA, :] = rest[w]


def log_decays(ref):
    table = ref[PAIR * D:PAIR * D + EXTRA, :].astype(F32)
    return [table[3 * j:3 * j + 1] + table[3 * j + 1:3 * j + 2] + table[3 * j + 2:3 * j + 3]
            for j in range(PAIR)]


def gather_row(own, r1, r2, r3, states, logs):
    x = (lax.axis_index("ctx") % SPAN) % ROW
    for step, ref in enumerate((own, r1, r2, r3)):
        w = (x - step + ROW) % ROW
        states[w] = ref[0:PAIR * D, :].astype(F32)
        for j, one in enumerate(log_decays(ref)):
            logs[w, 8 * j:8 * j + 8, :] = jnp.broadcast_to(one, (8, D))


def row_kernel(own, r1, r2, r3, out, states, logs):
    gather_row(own, r1, r2, r3, states, logs)
    at = iota((EXTRA, D), 0)
    table = jnp.zeros((EXTRA, D), F32)
    for j in range(PAIR):
        part = slice(j * D, (j + 1) * D)
        c = [logs[w, 8 * j:8 * j + 1, :] for w in range(ROW)]
        total = (states[3, part, :] + jnp.exp(c[3]) * states[2, part, :]
                 + jnp.exp(c[3] + c[2]) * states[1, part, :]
                 + jnp.exp(c[3] + c[2] + c[1]) * states[0, part, :])
        out[part, :] = total.astype(BF16)
        one = jnp.broadcast_to(c[0] + c[1] + c[2] + c[3], (EXTRA, D))
        a = one.astype(BF16).astype(F32)
        b = (one - a).astype(BF16).astype(F32)
        for i, x in enumerate((a, b, one - a - b)):
            table = jnp.where(at == 3 * j + i, x, table)
    out[PAIR * D:PAIR * D + EXTRA, :] = table.astype(BF16)


def prefix_kernel(own, r1, r2, r3, z1, z2, p0, p1, p2, p3, states, logs, ready):
    gather_row(own, r1, r2, r3, states, logs)
    decay = log_decays(z1)
    for j in range(PAIR):
        part = slice(j * D, (j + 1) * D)
        c = [logs[w, 8 * j:8 * j + 1, :] for w in range(ROW)]
        state = (z1[part, :].astype(F32) + jnp.exp(decay[j]) * z2[part, :].astype(F32))
        ready[0, part, :] = state.astype(BF16)
        state1 = states[0, part, :]
        ready[1, part, :] = (state1 + jnp.exp(c[0]) * state).astype(BF16)
        state2 = states[1, part, :] + jnp.exp(c[1]) * state1
        ready[2, part, :] = (state2 + jnp.exp(c[0] + c[1]) * state).astype(BF16)
        state3 = states[2, part, :] + jnp.exp(c[2]) * state2
        ready[3, part, :] = (state3 + jnp.exp(c[0] + c[1] + c[2]) * state).astype(BF16)
    x = (lax.axis_index("ctx") % SPAN) % ROW
    for step, out in enumerate((p0, p1, p2, p3)):
        out[...] = ready[(x + step) % ROW]


def intra_kernel(starts, lengths, query, key, value, cum, cum_t, out, bias):
    _, _, bound, _, _ = marks(starts, lengths)
    t = iota((T, T), 0)
    i = iota((T, T), 1)
    seen = (i <= t) & ((i >= bound) | (t < bound))
    bias[...] = jnp.where(seen, 0.0, NEG)
    for h in range(H):
        lanes = slice(h * D, (h + 1) * D)
        for r in range(T // D):
            part = slice(r * D, (r + 1) * D)
            wide = (r + 1) * D
            scores = lax.dot_general(query[part, lanes], key[0:wide, lanes], NT,
                                     preferred_element_type=F32)
            gap = (cum[part, h:h + 1] - cum_t[h:h + 1, 0:wide]) + bias[part, 0:wide]
            weights = (scores * jnp.exp(gap)).astype(BF16)
            out[part, lanes] = jnp.dot(weights, value[0:wide, lanes], preferred_element_type=F32)


def carry_kernel(starts, lengths, query, intra, p0, p1, p2, p3, cum, out, squares, states):
    _, place, bound, end_prev, end_cur = marks(starts, lengths)
    x = place % ROW
    for step, ref in enumerate((p0, p1, p2, p3)):
        states[(x - step + ROW) % ROW] = ref[...]
    rows = iota((T, 1), 0)
    valid = rows < jnp.where(rows < bound, end_prev, end_cur)
    enters = (rows < jnp.where(place > 0, T, bound)) & valid
    enter = jnp.where(enters, jnp.exp(cum[...]), 0.0)
    live = jnp.where(valid, 1.0, 0.0)
    acc = jnp.zeros((T, D), F32)
    for h in range(H):
        lanes = slice(h * D, (h + 1) * D)
        state = states[h // PAIR, (h % PAIR) * D:(h % PAIR + 1) * D, :]
        carried = jnp.dot(query[:, lanes], state, preferred_element_type=F32)
        heads = intra[:, lanes] * live + enter[:, h:h + 1] * carried
        out[:, lanes] = heads
        acc += heads * heads
    squares[...] = lax.dot_general(jnp.ones((8, D), F32), acc, NT, precision=HI,
                                   preferred_element_type=F32)


def norm_kernel(heads, gate, gain, squares, others, out, *, features):
    pick = (iota((8, D), 0) == 0).astype(F32)
    sums = lax.dot_general(squares[...] + others[...], pick, TN, precision=HI,
                           preferred_element_type=F32)
    scale = lax.rsqrt(sums * (1.0 / features) + EPS)
    for h in range(heads.shape[1] // D):
        lanes = slice(h * D, (h + 1) * D)
        gated = jax.nn.sigmoid(gate[:, lanes].astype(F32))
        out[:, lanes] = (heads[:, lanes] * scale * gain[:, lanes] * gated).astype(BF16)


def soft_kernel(starts, lengths, query, own, f1, f2, f3, f4, f5, f6, f7, f8, *rest, first):
    *done, out, keys, values, asks, top, acc = rest
    for ref in done:
        out[:, 0:first * D] = ref[...]
    room, place, bound, end_prev, end_cur = marks(starts, lengths)
    tail = place == 0
    count = jnp.where(tail, jnp.where(room > 0, SPAN, 0), place)
    begin_room = jnp.where(tail, jnp.maximum(room - 1, 0), room)
    begin = starts[begin_room] - begin_room * SPAN * T
    factor = (D ** -0.5) * 1.4426950408889634
    ones = jnp.ones((T, D), BF16)
    for m, ref in enumerate((own, f1, f2, f3, f4, f5, f6, f7, f8)):
        @pl.when(m <= count)
        def _():
            keys[m] = ref[:, 0:D]
            values[m, :, 0:D] = ref[:, D:2 * D]
            values[m, :, D:2 * D] = ones

    for h in range(PART):
        asks[h] = query[:, (first + h) * D:(first + h + 1) * D]

    def attend(m, size, hidden, fresh=False):
        k = keys[m]
        v = values[m]
        span = GROUP if size == T else 1
        many = span * size

        def ask(h):
            return lax.dot_general(asks[h:h + span, 0:size, :].reshape(many, D), k, NT,
                                   preferred_element_type=F32)

        heads = range(0, PART, span)
        ahead = ask(0)
        for h in heads:
            x = ahead
            if h + span < PART:
                ahead = ask(h + span)
            if hidden is not None:
                x = (x.reshape(span, size, T) + hidden[None]).reshape(many, T)
            parts = [x[:, j * D:(j + 1) * D] for j in range(T // D)]
            best = functools.reduce(jnp.maximum, parts)
            peak = jnp.broadcast_to(jnp.max(best, axis=1, keepdims=True), (many, D)) * factor
            if not fresh:
                old = top[h:h + span, 0:size, :].reshape(many, D)
                peak = jnp.maximum(old, peak)
                shrink = jnp.exp2(old - peak)
            top[h:h + span, 0:size, :] = peak.reshape(span, size, D)
            p = jnp.concatenate([jnp.exp2(y * factor - peak).astype(BF16) for y in parts], axis=1)
            mixed = jnp.dot(p, v, preferred_element_type=F32)
            if not fresh:
                kept = acc[h:h + span, 0:size, :].reshape(many, 2 * D)
                mixed = mixed + kept * jnp.concatenate([shrink, shrink], axis=1)
            acc[h:h + span, 0:size, :] = mixed.reshape(span, size, 2 * D)

    t = iota((T, T), 0)
    i = iota((T, T), 1)
    seen = (i <= t) & ((i >= bound) | (t < bound))
    attend(0, T, jnp.where(seen, 0.0, NEG), fresh=True)

    @pl.when(place > 0)
    def _():
        def middle(m, _):
            attend(m, T, None)
            return 0

        lax.fori_loop(1, count, middle, 0)
        attend(count, T, jnp.where(iota((1, T), 1) < begin, NEG, 0.0))

    half = T // 2

    @pl.when(tail & (count > 0))
    def _():
        def one(m, _):
            row_ok = iota((half, T), 0) < bound
            first_key = jnp.where(m == count, begin, 0)
            attend(m, half, jnp.where(row_ok & (iota((half, T), 1) >= first_key), 0.0, NEG))
            return 0

        lax.fori_loop(1, count + 1, one, 0)

    valid = valid_rows((T, 1), bound, end_prev, end_cur)
    for h in range(PART):
        mixed = acc[h, :, 0:D] / acc[h, :, D:2 * D]
        out[:, (first + h) * D:(first + h + 1) * D] = jnp.where(valid, mixed, 0.0).astype(BF16)


smem = pl.BlockSpec(memory_space=pltpu.SMEM)
vmem = pl.BlockSpec(memory_space=pltpu.VMEM)


def shape(*dims, kind=F32):
    return jax.ShapeDtypeStruct(dims, kind)


def call(kernel, tables, operands, outs, scratch=(), room=12):
    return pl.pallas_call(
        kernel, in_specs=[smem] * tables + [vmem] * (len(operands) - tables),
        out_specs=[vmem] * len(outs), out_shape=list(outs), scratch_shapes=list(scratch),
        compiler_params=pltpu.CompilerParams(
            vmem_limit_bytes=room << 20),
    )(*operands)


def window(distance, rooms):
    pairs = []
    for room in range(rooms):
        base = room * SPAN
        for i in range(base, base + SPAN):
            j = i + distance
            if j <= base + SPAN and j < rooms * SPAN:
                pairs.append((i, j))
    return pairs


def per_device(lin_query, lin_key, lin_value, lin_gate, lin_decay, norm_gain,
               soft_query, soft_key, soft_value, starts, lengths):
    places = lax.axis_size("ctx")
    rooms = places // SPAN
    share = lax.axis_size("head")
    width = H * D
    piece = PAIR * D
    around = [[(i, i - i % ROW + (i + step) % ROW) for i in range(places)] for step in range(ROW)]
    onward = [(i, i + ROW) for i in range(places - ROW)]
    beyond = [(i, i + 2 * ROW) for i in range(places - 2 * ROW) if i // ROW % 2 == 0]

    def send(x, pairs):
        return lax.ppermute(x, "ctx", pairs)

    packed = shape(piece + EXTRA, D, kind=BF16)

    pair = shape(T, 2 * D, kind=BF16)
    *slices, cum, cum_t, kv = call(
        state_kernel, 2,
        (starts, lengths, lin_key, lin_value, lin_decay.T, soft_key, soft_value),
        [packed] * ROW + [shape(T, H), shape(H, T), pair],
        [pltpu.VMEM((ROW, piece, D), BF16), pltpu.VMEM((ROW, EXTRA, D), BF16)])
    row = [slices[0]] + [send(slices[j], around[j]) for j in range(1, ROW)]

    intra, = call(intra_kernel, 2,
                  (starts, lengths, lin_query, lin_key, lin_value, cum, cum_t),
                  [shape(T, width)], [pltpu.VMEM((T, T), F32)])

    table = [pltpu.VMEM((ROW, piece, D), F32), pltpu.VMEM((ROW, 8 * PAIR, D), F32)]
    row_total, = call(row_kernel, 0, row, [packed], table)
    above = send(row_total, onward)
    above2 = send(row_total, beyond)
    ready = call(
        prefix_kernel, 0, (*row, above, above2), [shape(piece, D, kind=BF16)] * ROW,
        table + [pltpu.VMEM((ROW, piece, D), BF16)])
    before = [ready[0]] + [send(ready[j], around[j]) for j in range(1, ROW)]

    far_kv = [send(kv, window(m, rooms)) for m in range(1, SPAN + 1)]

    heads, squares = call(
        carry_kernel, 2, (starts, lengths, lin_query, intra, *before, cum),
        [shape(T, width), shape(8, T)], [pltpu.VMEM((ROW, piece, D), BF16)])
    step = 1
    others = jnp.zeros_like(squares)
    while step < share:
        if step > 1:
            squares = squares + others
        others = lax.ppermute(squares, "head", [(i, i ^ step) for i in range(share)])
        step *= 2

    done = []
    for first in range(0, H, PART):
        done = call(
            functools.partial(soft_kernel, first=first), 2,
            (starts, lengths, soft_query, kv, *far_kv, *done),
            [shape(T, (first + PART) * D, kind=BF16)],
            [pltpu.VMEM((SPAN + 1, T, D), BF16), pltpu.VMEM((SPAN + 1, T, 2 * D), BF16),
             pltpu.VMEM((PART, T, D), BF16), pltpu.VMEM((PART, T, D), F32),
             pltpu.VMEM((PART, T, 2 * D), F32)], room=20)
    soft_out, = done

    lin_out, = call(
        functools.partial(norm_kernel, features=width * share), 0,
        (heads, lin_gate, norm_gain.reshape(1, width), squares, others),
        [shape(T, width, kind=BF16)])
    return (lin_out, soft_out)


def solution(mesh):
    wide = P("ctx", "head")
    return jax.shard_map(
        per_device, mesh=mesh,
        in_specs=(wide, wide, wide, wide, wide, P("head"), wide, wide, wide, P(), P()),
        out_specs=(wide, wide), check_vma=False,
    )
```

```python
import functools
import jax
import jax.numpy as jnp
from jax import lax
from jax.experimental import pallas as pl
from jax.experimental.pallas import tpu as pltpu
from jax.sharding import PartitionSpec as P


T = 384
D = 128
H = 8
SPAN = 8
NEG = -1e30
FAR = 4
GROUP = 2
EPS = 1e-06
GONE = -1e5
ROW = 4
PAIR = H // ROW
EXTRA = 16
HI = lax.Precision.HIGHEST
F32 = jnp.float32
BF16 = jnp.bfloat16
NT = (((1,), (1,)), ((), ()))
TN = (((0,), (0,)), ((), ()))


def iota(shape, axis):
    return lax.broadcasted_iota(jnp.int32, shape, axis)


def marks(starts, lengths):
    device = lax.axis_index("ctx")
    room = device // SPAN
    place = device % SPAN
    first = device * T
    at_start = place == 0
    bound = jnp.where(at_start, starts[room] - first, 0)
    earlier = jnp.maximum(room - 1, 0)
    end_prev = jnp.where(at_start & (room > 0), starts[earlier] + lengths[earlier] - first, 0)
    end_cur = starts[room] + lengths[room] - first
    return room, place, bound, end_prev, end_cur


def valid_rows(shape, bound, end_prev, end_cur):
    rows = iota(shape, 0)
    return rows < jnp.where(rows < bound, end_prev, end_cur)


def state_kernel(starts_in, lengths_in, dec_in, key_in, value_in, soft_key, soft_value,
                 s0, s1, s2, s3, cum, cum_t, both,
                 starts, lengths, dec_t, key, value, pack, rest, sems):
    moves = ((dec_in, dec_t), (starts_in, starts), (lengths_in, lengths), (key_in, key),
             (value_in, value), (soft_key, both.at[:, 0:D]), (soft_value, both.at[:, D:2 * D]))
    copies = [pltpu.make_async_copy(a, b, sems.at[n]) for n, (a, b) in enumerate(moves)]
    for copy in copies:
        copy.start()
    for copy in copies[:3]:
        copy.wait()
    _, place, bound, _, end_cur = marks(starts, lengths)
    lower = (iota((T, T), 1) <= iota((T, T), 0)).astype(F32)
    dec = dec_t[...]
    col = lax.dot_general(lower, dec, NT, precision=HI, preferred_element_type=F32)
    cum[...] = col
    cum_t[...] = lax.dot_general(dec, lower, NT, precision=HI, preferred_element_type=F32)
    rows = iota((T, 1), 0)
    keep = (rows >= bound) & (rows < end_cur)
    last = col[T - 1:T, :]
    to_end = jnp.where(keep, jnp.exp(last - col), 0.0)
    total = jnp.where(place == 0, GONE, last)
    for copy in copies[3:]:
        copy.wait()
    for h in range(H):
        part = slice(h * D, (h + 1) * D)
        scaled = (key[:, part].astype(F32) * to_end[:, h:h + 1]).astype(BF16)
        state = lax.dot_general(scaled, value[:, part], TN, preferred_element_type=F32)
        pack[h // PAIR, (h % PAIR) * D:(h % PAIR + 1) * D, :] = state.astype(BF16)
    at = iota((EXTRA, D), 0)
    for w in range(ROW):
        table = jnp.zeros((EXTRA, D), F32)
        for j in range(PAIR):
            one = jnp.broadcast_to(total[:, w * PAIR + j:w * PAIR + j + 1], (EXTRA, D))
            a = one.astype(BF16).astype(F32)
            b = (one - a).astype(BF16).astype(F32)
            c = one - a - b
            for i, x in enumerate((a, b, c)):
                table = jnp.where(at == 3 * j + i, x, table)
        rest[w] = table.astype(BF16)
    x = place % ROW
    for step, out in enumerate((s0, s1, s2, s3)):
        w = (x + step) % ROW
        out[0:PAIR * D, :] = pack[w]
        out[PAIR * D:PAIR * D + EXTRA, :] = rest[w]


def log_decays(ref):
    table = ref[PAIR * D:PAIR * D + EXTRA, :].astype(F32)
    return [table[3 * j:3 * j + 1] + table[3 * j + 1:3 * j + 2] + table[3 * j + 2:3 * j + 3]
            for j in range(PAIR)]


def gather_row(own, r1, r2, r3, states, logs):
    x = (lax.axis_index("ctx") % SPAN) % ROW
    for step, ref in enumerate((own, r1, r2, r3)):
        w = (x - step + ROW) % ROW
        states[w] = ref[0:PAIR * D, :].astype(F32)
        for j, one in enumerate(log_decays(ref)):
            logs[w, 8 * j:8 * j + 8, :] = jnp.broadcast_to(one, (8, D))


def row_kernel(own, r1, r2, r3, out, states, logs):
    gather_row(own, r1, r2, r3, states, logs)
    at = iota((EXTRA, D), 0)
    table = jnp.zeros((EXTRA, D), F32)
    for j in range(PAIR):
        part = slice(j * D, (j + 1) * D)
        c = [logs[w, 8 * j:8 * j + 1, :] for w in range(ROW)]
        total = (states[3, part, :] + jnp.exp(c[3]) * states[2, part, :]
                 + jnp.exp(c[3] + c[2]) * states[1, part, :]
                 + jnp.exp(c[3] + c[2] + c[1]) * states[0, part, :])
        out[part, :] = total.astype(BF16)
        one = jnp.broadcast_to(c[0] + c[1] + c[2] + c[3], (EXTRA, D))
        a = one.astype(BF16).astype(F32)
        b = (one - a).astype(BF16).astype(F32)
        for i, x in enumerate((a, b, one - a - b)):
            table = jnp.where(at == 3 * j + i, x, table)
    out[PAIR * D:PAIR * D + EXTRA, :] = table.astype(BF16)


def prefix_kernel(own, r1, r2, r3, z1, z2, p0, p1, p2, p3, states, logs, ready):
    gather_row(own, r1, r2, r3, states, logs)
    decay = log_decays(z1)
    for j in range(PAIR):
        part = slice(j * D, (j + 1) * D)
        c = [logs[w, 8 * j:8 * j + 1, :] for w in range(ROW)]
        state = (z1[part, :].astype(F32) + jnp.exp(decay[j]) * z2[part, :].astype(F32))
        ready[0, part, :] = state.astype(BF16)
        state1 = states[0, part, :]
        ready[1, part, :] = (state1 + jnp.exp(c[0]) * state).astype(BF16)
        state2 = states[1, part, :] + jnp.exp(c[1]) * state1
        ready[2, part, :] = (state2 + jnp.exp(c[0] + c[1]) * state).astype(BF16)
        state3 = states[2, part, :] + jnp.exp(c[2]) * state2
        ready[3, part, :] = (state3 + jnp.exp(c[0] + c[1] + c[2]) * state).astype(BF16)
    x = (lax.axis_index("ctx") % SPAN) % ROW
    for step, out in enumerate((p0, p1, p2, p3)):
        out[...] = ready[(x + step) % ROW]


def intra_kernel(starts, lengths, query, key, value, cum, cum_t, out, bias):
    _, _, bound, _, _ = marks(starts, lengths)
    t = iota((T, T), 0)
    i = iota((T, T), 1)
    seen = (i <= t) & ((i >= bound) | (t < bound))
    bias[...] = jnp.where(seen, 0.0, NEG)
    for h in range(H):
        lanes = slice(h * D, (h + 1) * D)
        for r in range(T // D):
            part = slice(r * D, (r + 1) * D)
            wide = (r + 1) * D
            scores = lax.dot_general(query[part, lanes], key[0:wide, lanes], NT,
                                     preferred_element_type=F32)
            gap = (cum[part, h:h + 1] - cum_t[h:h + 1, 0:wide]) + bias[part, 0:wide]
            weights = (scores * jnp.exp(gap)).astype(BF16)
            out[part, lanes] = jnp.dot(weights, value[0:wide, lanes], preferred_element_type=F32)


def carry_kernel(starts, lengths, query, intra, p0, p1, p2, p3, cum, out, squares, states):
    _, place, bound, end_prev, end_cur = marks(starts, lengths)
    x = place % ROW
    for step, ref in enumerate((p0, p1, p2, p3)):
        states[(x - step + ROW) % ROW] = ref[...]
    rows = iota((T, 1), 0)
    valid = rows < jnp.where(rows < bound, end_prev, end_cur)
    enters = (rows < jnp.where(place > 0, T, bound)) & valid
    enter = jnp.where(enters, jnp.exp(cum[...]), 0.0)
    live = jnp.where(valid, 1.0, 0.0)
    acc = jnp.zeros((T, D), F32)
    for h in range(H):
        lanes = slice(h * D, (h + 1) * D)
        state = states[h // PAIR, (h % PAIR) * D:(h % PAIR + 1) * D, :]
        carried = jnp.dot(query[:, lanes], state, preferred_element_type=F32)
        heads = intra[:, lanes] * live + enter[:, h:h + 1] * carried
        out[:, lanes] = heads
        acc += heads * heads
    squares[...] = lax.dot_general(jnp.ones((8, D), F32), acc, NT, precision=HI,
                                   preferred_element_type=F32)


def norm_kernel(heads, gate, gain, squares, others, out, *, features):
    pick = (iota((8, D), 0) == 0).astype(F32)
    sums = lax.dot_general(squares[...] + others[...], pick, TN, precision=HI,
                           preferred_element_type=F32)
    scale = lax.rsqrt(sums * (1.0 / features) + EPS)
    for h in range(heads.shape[1] // D):
        lanes = slice(h * D, (h + 1) * D)
        gated = jax.nn.sigmoid(gate[:, lanes].astype(F32))
        out[:, lanes] = (heads[:, lanes] * scale * gain[:, lanes] * gated).astype(BF16)


def soft_kernel(starts, lengths, query, own, *rest, low, last):
    far = rest[:FAR]
    if last:
        top_in, acc_in, out, keys, values, asks, top, acc = rest[FAR:]
        top[...] = top_in[...]
        acc[...] = acc_in[...]
    else:
        top, acc, keys, values, asks = rest[FAR:]
    room, place, bound, end_prev, end_cur = marks(starts, lengths)
    tail = place == 0
    count = jnp.where(tail, jnp.where(room > 0, SPAN, 0), place)
    begin_room = jnp.where(tail, jnp.maximum(room - 1, 0), room)
    begin = starts[begin_room] - begin_room * SPAN * T
    factor = (D ** -0.5) * 1.4426950408889634
    ones = jnp.ones((T, D), BF16)
    for slot, ref in enumerate((own,) + far):
        @pl.when((slot + low - 1 <= count) if slot else (low == 1))
        def _():
            keys[slot] = ref[:, 0:D]
            values[slot, :, 0:D] = ref[:, D:2 * D]
            values[slot, :, D:2 * D] = ones

    for h in range(H):
        asks[h] = query[:, h * D:(h + 1) * D]

    def attend(slot, size, hidden, fresh=False):
        k = keys[slot]
        v = values[slot]
        span = GROUP if size == T else 1
        many = span * size

        def ask(h):
            return lax.dot_general(asks[h:h + span, 0:size, :].reshape(many, D), k, NT,
                                   preferred_element_type=F32)

        ahead = ask(0)
        for h in range(0, H, span):
            x = ahead
            if h + span < H:
                ahead = ask(h + span)
            x = (x.reshape(span, size, T) + hidden[None]).reshape(many, T)
            parts = [x[:, j * D:(j + 1) * D] for j in range(T // D)]
            best = functools.reduce(jnp.maximum, parts)
            peak = jnp.broadcast_to(jnp.max(best, axis=1, keepdims=True), (many, D)) * factor
            if not fresh:
                old = top[h:h + span, 0:size, :].reshape(many, D)
                peak = jnp.maximum(old, peak)
                shrink = jnp.exp2(old - peak)
            top[h:h + span, 0:size, :] = peak.reshape(span, size, D)
            p = jnp.concatenate([jnp.exp2(y * factor - peak).astype(BF16) for y in parts], axis=1)
            mixed = jnp.dot(p, v, preferred_element_type=F32)
            if not fresh:
                kept = acc[h:h + span, 0:size, :].reshape(many, 2 * D)
                mixed = mixed + kept * jnp.concatenate([shrink, shrink], axis=1)
            acc[h:h + span, 0:size, :] = mixed.reshape(span, size, 2 * D)

    if low == 1:
        t = iota((T, T), 0)
        i = iota((T, T), 1)
        seen = (i <= t) & ((i >= bound) | (t < bound))
        attend(0, T, jnp.where(seen, 0.0, NEG), fresh=True)
    slots = jnp.minimum(count, low + FAR - 1) - low + 2

    def first_key(slot):
        return jnp.where(slot + low - 1 == count, begin, 0)

    @pl.when(place > 0)
    def _():
        def one(slot, _):
            attend(slot, T, jnp.where(iota((1, T), 1) < first_key(slot), NEG, 0.0))
            return 0

        lax.fori_loop(1, slots, one, 0)

    half = T // 2

    @pl.when(tail & (count > 0))
    def _():
        def one(slot, _):
            seen = (iota((half, T), 0) < bound) & (iota((half, T), 1) >= first_key(slot))
            attend(slot, half, jnp.where(seen, 0.0, NEG))
            return 0

        lax.fori_loop(1, slots, one, 0)

    if last:
        valid = valid_rows((T, 1), bound, end_prev, end_cur)
        for h in range(H):
            mixed = acc[h, :, 0:D] / acc[h, :, D:2 * D]
            out[:, h * D:(h + 1) * D] = jnp.where(valid, mixed, 0.0).astype(BF16)


smem = pl.BlockSpec(memory_space=pltpu.SMEM)
vmem = pl.BlockSpec(memory_space=pltpu.VMEM)
hbm = pl.BlockSpec(memory_space=pltpu.HBM)


def shape(*dims, kind=F32):
    return jax.ShapeDtypeStruct(dims, kind)


def call(kernel, tables, operands, outs, scratch=(), room=12, given=vmem):
    return pl.pallas_call(
        kernel, in_specs=[smem] * tables + [given] * (len(operands) - tables),
        out_specs=[vmem] * len(outs), out_shape=list(outs), scratch_shapes=list(scratch),
        compiler_params=pltpu.CompilerParams(
            vmem_limit_bytes=room << 20),
    )(*operands)


def window(distance, rooms):
    pairs = []
    for room in range(rooms):
        base = room * SPAN
        for i in range(base, base + SPAN):
            j = i + distance
            if j <= base + SPAN and j < rooms * SPAN:
                pairs.append((i, j))
    return pairs


def per_device(lin_query, lin_key, lin_value, lin_gate, lin_decay, norm_gain,
               soft_query, soft_key, soft_value, starts, lengths):
    places = lax.axis_size("ctx")
    rooms = places // SPAN
    share = lax.axis_size("head")
    width = H * D
    piece = PAIR * D
    around = [[(i, i - i % ROW + (i + step) % ROW) for i in range(places)] for step in range(ROW)]
    onward = [(i, i + ROW) for i in range(places - ROW)]
    beyond = [(i, i + 2 * ROW) for i in range(places - 2 * ROW) if i // ROW % 2 == 0]

    def send(x, pairs):
        return lax.ppermute(x, "ctx", pairs)

    packed = shape(piece + EXTRA, D, kind=BF16)

    pair = shape(T, 2 * D, kind=BF16)
    *slices, cum, cum_t, kv = call(
        state_kernel, 0,
        [pltpu.with_memory_space_constraint(x, pltpu.HBM) for x in
         (starts, lengths, lin_decay.T, lin_key, lin_value, soft_key, soft_value)],
        [packed] * ROW + [shape(T, H), shape(H, T), pair],
        [pltpu.SMEM(starts.shape, jnp.int32), pltpu.SMEM(lengths.shape, jnp.int32),
         pltpu.VMEM((H, T), F32), pltpu.VMEM((T, width), BF16), pltpu.VMEM((T, width), BF16),
         pltpu.VMEM((ROW, piece, D), BF16), pltpu.VMEM((ROW, EXTRA, D), BF16),
         pltpu.SemaphoreType.DMA((7,))], given=hbm)
    row = [slices[0]] + [send(slices[j], around[j]) for j in range(1, ROW)]

    intra, = call(intra_kernel, 2,
                  (starts, lengths, lin_query, lin_key, lin_value, cum, cum_t),
                  [shape(T, width)], [pltpu.VMEM((T, T), F32)])

    table = [pltpu.VMEM((ROW, piece, D), F32), pltpu.VMEM((ROW, 8 * PAIR, D), F32)]
    row_total, = call(row_kernel, 0, row, [packed], table)
    above = send(row_total, onward)
    above2 = send(row_total, beyond)
    ready = call(
        prefix_kernel, 0, (*row, above, above2), [shape(piece, D, kind=BF16)] * ROW,
        table + [pltpu.VMEM((ROW, piece, D), BF16)])
    before = [ready[0]] + [send(ready[j], around[j]) for j in range(1, ROW)]

    far_kv = [send(kv, window(m, rooms)) for m in range(1, ROW + 1)]
    far_kv += [send(far_kv[ROW - 1], [(i + ROW, j) for i, j in window(m, rooms)])
               for m in range(ROW + 1, SPAN + 1)]

    heads, squares = call(
        carry_kernel, 2, (starts, lengths, lin_query, intra, *before, cum),
        [shape(T, width), shape(8, T)], [pltpu.VMEM((ROW, piece, D), BF16)])
    step = 1
    others = jnp.zeros_like(squares)
    while step < share:
        if step > 1:
            squares = squares + others
        others = lax.ppermute(squares, "head", [(i, i ^ step) for i in range(share)])
        step *= 2

    held = [shape(H, T, D), shape(H, T, 2 * D)]
    room = [pltpu.VMEM((FAR + 1, T, D), BF16), pltpu.VMEM((FAR + 1, T, 2 * D), BF16),
            pltpu.VMEM((H, T, D), BF16)]
    asked = (starts, lengths, soft_query, kv)
    running = call(functools.partial(soft_kernel, low=1, last=False), 2,
                   (*asked, *far_kv[:FAR]), held, room, room=20)
    soft_out, = call(functools.partial(soft_kernel, low=FAR + 1, last=True), 2,
                     (*asked, *far_kv[FAR:], *running), [shape(T, width, kind=BF16)],
                     room + [pltpu.VMEM(x.shape, F32) for x in held], room=24)

    lin_out, = call(
        functools.partial(norm_kernel, features=width * share), 0,
        (heads, lin_gate, norm_gain.reshape(1, width), squares, others),
        [shape(T, width, kind=BF16)])
    return (lin_out, soft_out)


def solution(mesh):
    wide = P("ctx", "head")
    return jax.shard_map(
        per_device, mesh=mesh,
        in_specs=(wide, wide, wide, wide, wide, P("head"), wide, wide, wide, P(), P()),
        out_specs=(wide, wide), check_vma=False,
    )
```

```python
import functools
import jax
import jax.numpy as jnp
from jax import lax
from jax.experimental import pallas as pl
from jax.experimental.pallas import tpu as pltpu
from jax.sharding import PartitionSpec as P


T = 384
D = 128
H = 8
SPAN = 8
NEG = -1e30
FAR = 4
GROUP = 2
EPS = 1e-06
GONE = -1e5
ROW = 4
PAIR = H // ROW
EXTRA = 16
HI = lax.Precision.HIGHEST
F32 = jnp.float32
BF16 = jnp.bfloat16
NT = (((1,), (1,)), ((), ()))
TN = (((0,), (0,)), ((), ()))


def iota(shape, axis):
    return lax.broadcasted_iota(jnp.int32, shape, axis)


def marks(starts, lengths):
    device = lax.axis_index("ctx")
    room = device // SPAN
    place = device % SPAN
    first = device * T
    at_start = place == 0
    bound = jnp.where(at_start, starts[room] - first, 0)
    earlier = jnp.maximum(room - 1, 0)
    end_prev = jnp.where(at_start & (room > 0), starts[earlier] + lengths[earlier] - first, 0)
    end_cur = starts[room] + lengths[room] - first
    return room, place, bound, end_prev, end_cur


def valid_rows(shape, bound, end_prev, end_cur):
    rows = iota(shape, 0)
    return rows < jnp.where(rows < bound, end_prev, end_cur)


def state_kernel(starts_in, lengths_in, dec_in, key_in, value_in, soft_key, soft_value,
                 s0, s1, s2, s3, cum, cum_t, both,
                 starts, lengths, dec_t, key, value, pack, rest, sems):
    moves = ((dec_in, dec_t), (starts_in, starts), (lengths_in, lengths), (key_in, key),
             (value_in, value), (soft_key, both.at[:, 0:D]), (soft_value, both.at[:, D:2 * D]))
    copies = [pltpu.make_async_copy(a, b, sems.at[n]) for n, (a, b) in enumerate(moves)]
    for copy in copies:
        copy.start()
    for copy in copies[:3]:
        copy.wait()
    _, place, bound, _, end_cur = marks(starts, lengths)
    lower = (iota((T, T), 1) <= iota((T, T), 0)).astype(F32)
    dec = dec_t[...]
    col = lax.dot_general(lower, dec, NT, precision=HI, preferred_element_type=F32)
    cum[...] = col
    cum_t[...] = lax.dot_general(dec, lower, NT, precision=HI, preferred_element_type=F32)
    rows = iota((T, 1), 0)
    keep = (rows >= bound) & (rows < end_cur)
    last = col[T - 1:T, :]
    to_end = jnp.where(keep, jnp.exp(last - col), 0.0)
    total = jnp.where(place == 0, GONE, last)
    for copy in copies[3:]:
        copy.wait()
    for h in range(H):
        part = slice(h * D, (h + 1) * D)
        scaled = (key[:, part].astype(F32) * to_end[:, h:h + 1]).astype(BF16)
        state = lax.dot_general(scaled, value[:, part], TN, preferred_element_type=F32)
        pack[h // PAIR, (h % PAIR) * D:(h % PAIR + 1) * D, :] = state.astype(BF16)
    at = iota((EXTRA, D), 0)
    for w in range(ROW):
        table = jnp.zeros((EXTRA, D), F32)
        for j in range(PAIR):
            one = jnp.broadcast_to(total[:, w * PAIR + j:w * PAIR + j + 1], (EXTRA, D))
            a = one.astype(BF16).astype(F32)
            b = (one - a).astype(BF16).astype(F32)
            c = one - a - b
            for i, x in enumerate((a, b, c)):
                table = jnp.where(at == 3 * j + i, x, table)
        rest[w] = table.astype(BF16)
    x = place % ROW
    for step, out in enumerate((s0, s1, s2, s3)):
        w = (x + step) % ROW
        out[0:PAIR * D, :] = pack[w]
        out[PAIR * D:PAIR * D + EXTRA, :] = rest[w]


def log_decays(ref):
    table = ref[PAIR * D:PAIR * D + EXTRA, :].astype(F32)
    return [table[3 * j:3 * j + 1] + table[3 * j + 1:3 * j + 2] + table[3 * j + 2:3 * j + 3]
            for j in range(PAIR)]


def gather_row(own, r1, r2, r3, states, logs):
    x = (lax.axis_index("ctx") % SPAN) % ROW
    for step, ref in enumerate((own, r1, r2, r3)):
        w = (x - step + ROW) % ROW
        states[w] = ref[0:PAIR * D, :].astype(F32)
        for j, one in enumerate(log_decays(ref)):
            logs[w, 8 * j:8 * j + 8, :] = jnp.broadcast_to(one, (8, D))


def row_kernel(own, r1, r2, r3, out, states, logs):
    gather_row(own, r1, r2, r3, states, logs)
    for j in range(PAIR):
        part = slice(j * D, (j + 1) * D)
        c = [logs[w, 8 * j:8 * j + 1, :] for w in range(ROW)]
        total = (states[3, part, :] + jnp.exp(c[3]) * states[2, part, :]
                 + jnp.exp(c[3] + c[2]) * states[1, part, :]
                 + jnp.exp(c[3] + c[2] + c[1]) * states[0, part, :])
        out[part, :] = total.astype(BF16)


def prefix_kernel(own, r1, r2, r3, above, p0, p1, p2, p3, states, logs, ready):
    gather_row(own, r1, r2, r3, states, logs)
    for j in range(PAIR):
        part = slice(j * D, (j + 1) * D)
        c = [logs[w, 8 * j:8 * j + 1, :] for w in range(ROW)]
        state = above[part, :].astype(F32)
        ready[0, part, :] = state.astype(BF16)
        state1 = states[0, part, :]
        ready[1, part, :] = (state1 + jnp.exp(c[0]) * state).astype(BF16)
        state2 = states[1, part, :] + jnp.exp(c[1]) * state1
        ready[2, part, :] = (state2 + jnp.exp(c[0] + c[1]) * state).astype(BF16)
        state3 = states[2, part, :] + jnp.exp(c[2]) * state2
        ready[3, part, :] = (state3 + jnp.exp(c[0] + c[1] + c[2]) * state).astype(BF16)
    x = (lax.axis_index("ctx") % SPAN) % ROW
    for step, out in enumerate((p0, p1, p2, p3)):
        out[...] = ready[(x + step) % ROW]


def pass_kernel(s0, s1, s2, s3, p0, p1, p2, p3, out):
    x = (lax.axis_index("ctx") % SPAN) % ROW
    entering = (p0, p3, p2, p1)
    for step, ref in enumerate((s0, s1, s2, s3)):
        w = (x + step) % ROW
        logs = log_decays(ref)
        for j in range(PAIR):
            part = slice(j * D, (j + 1) * D)
            state = (ref[part, :].astype(F32)
                     + jnp.exp(logs[j]) * entering[step][part, :].astype(F32))
            out[w, part, :] = state.astype(BF16)


def intra_kernel(starts, lengths, query, key, value, cum, cum_t, out, bias):
    _, _, bound, _, _ = marks(starts, lengths)
    t = iota((T, T), 0)
    i = iota((T, T), 1)
    seen = (i <= t) & ((i >= bound) | (t < bound))
    bias[...] = jnp.where(seen, 0.0, NEG)
    for h in range(H):
        lanes = slice(h * D, (h + 1) * D)
        for r in range(T // D):
            part = slice(r * D, (r + 1) * D)
            wide = (r + 1) * D
            scores = lax.dot_general(query[part, lanes], key[0:wide, lanes], NT,
                                     preferred_element_type=F32)
            gap = (cum[part, h:h + 1] - cum_t[h:h + 1, 0:wide]) + bias[part, 0:wide]
            weights = (scores * jnp.exp(gap)).astype(BF16)
            out[part, lanes] = jnp.dot(weights, value[0:wide, lanes], preferred_element_type=F32)


def carry_kernel(starts, lengths, query, intra, p0, p1, p2, p3, passed, cum, out, squares,
                 states):
    _, place, bound, end_prev, end_cur = marks(starts, lengths)
    x = place % ROW
    for step, ref in enumerate((p0, p1, p2, p3)):
        states[(x - step + ROW) % ROW] = ref[...]

    @pl.when(place == 0)
    def _():
        states[...] = passed[...]

    rows = iota((T, 1), 0)
    valid = rows < jnp.where(rows < bound, end_prev, end_cur)
    enters = (rows < jnp.where(place > 0, T, bound)) & valid
    enter = jnp.where(enters, jnp.exp(cum[...]), 0.0)
    live = jnp.where(valid, 1.0, 0.0)
    acc = jnp.zeros((T, D), F32)
    for h in range(H):
        lanes = slice(h * D, (h + 1) * D)
        state = states[h // PAIR, (h % PAIR) * D:(h % PAIR + 1) * D, :]
        carried = jnp.dot(query[:, lanes], state, preferred_element_type=F32)
        heads = intra[:, lanes] * live + enter[:, h:h + 1] * carried
        out[:, lanes] = heads
        acc += heads * heads
    squares[...] = lax.dot_general(jnp.ones((8, D), F32), acc, NT, precision=HI,
                                   preferred_element_type=F32)


def norm_kernel(heads, gate, gain, squares, others, out, *, features):
    pick = (iota((8, D), 0) == 0).astype(F32)
    sums = lax.dot_general(squares[...] + others[...], pick, TN, precision=HI,
                           preferred_element_type=F32)
    scale = lax.rsqrt(sums * (1.0 / features) + EPS)
    for h in range(heads.shape[1] // D):
        lanes = slice(h * D, (h + 1) * D)
        gated = jax.nn.sigmoid(gate[:, lanes].astype(F32))
        out[:, lanes] = (heads[:, lanes] * scale * gain[:, lanes] * gated).astype(BF16)


def soft_kernel(starts, lengths, query, own, *rest, low, last):
    far = rest[:FAR]
    if last:
        top_in, acc_in, out, keys, values, asks, top, acc = rest[FAR:]
        top[...] = top_in[...]
        acc[...] = acc_in[...]
    else:
        top, acc, keys, values, asks = rest[FAR:]
    room, place, bound, end_prev, end_cur = marks(starts, lengths)
    tail = place == 0
    count = jnp.where(tail, jnp.where(room > 0, SPAN, 0), place)
    begin_room = jnp.where(tail, jnp.maximum(room - 1, 0), room)
    begin = starts[begin_room] - begin_room * SPAN * T
    factor = (D ** -0.5) * 1.4426950408889634
    ones = jnp.ones((T, D), BF16)
    for slot, ref in enumerate((own,) + far):
        @pl.when((slot + low - 1 <= count) if slot else (low == 1))
        def _():
            keys[slot] = ref[:, 0:D]
            values[slot, :, 0:D] = ref[:, D:2 * D]
            values[slot, :, D:2 * D] = ones

    for h in range(H):
        asks[h] = query[:, h * D:(h + 1) * D]

    def attend(slot, size, hidden, fresh=False):
        k = keys[slot]
        v = values[slot]
        span = GROUP if size == T else 1
        many = span * size

        def ask(h):
            return lax.dot_general(asks[h:h + span, 0:size, :].reshape(many, D), k, NT,
                                   preferred_element_type=F32)

        ahead = ask(0)
        for h in range(0, H, span):
            x = ahead
            if h + span < H:
                ahead = ask(h + span)
            x = (x.reshape(span, size, T) + hidden[None]).reshape(many, T)
            parts = [x[:, j * D:(j + 1) * D] for j in range(T // D)]
            best = functools.reduce(jnp.maximum, parts)
            peak = jnp.broadcast_to(jnp.max(best, axis=1, keepdims=True), (many, D)) * factor
            if not fresh:
                old = top[h:h + span, 0:size, :].reshape(many, D)
                peak = jnp.maximum(old, peak)
                shrink = jnp.exp2(old - peak)
            top[h:h + span, 0:size, :] = peak.reshape(span, size, D)
            p = jnp.concatenate([jnp.exp2(y * factor - peak).astype(BF16) for y in parts], axis=1)
            mixed = jnp.dot(p, v, preferred_element_type=F32)
            if not fresh:
                kept = acc[h:h + span, 0:size, :].reshape(many, 2 * D)
                mixed = mixed + kept * jnp.concatenate([shrink, shrink], axis=1)
            acc[h:h + span, 0:size, :] = mixed.reshape(span, size, 2 * D)

    if low == 1:
        t = iota((T, T), 0)
        i = iota((T, T), 1)
        seen = (i <= t) & ((i >= bound) | (t < bound))
        attend(0, T, jnp.where(seen, 0.0, NEG), fresh=True)
    slots = jnp.minimum(count, low + FAR - 1) - low + 2

    def first_key(slot):
        return jnp.where(slot + low - 1 == count, begin, 0)

    @pl.when(place > 0)
    def _():
        def one(slot, _):
            attend(slot, T, jnp.where(iota((1, T), 1) < first_key(slot), NEG, 0.0))
            return 0

        lax.fori_loop(1, slots, one, 0)

    half = T // 2

    @pl.when(tail & (count > 0))
    def _():
        def one(slot, _):
            seen = (iota((half, T), 0) < bound) & (iota((half, T), 1) >= first_key(slot))
            attend(slot, half, jnp.where(seen, 0.0, NEG))
            return 0

        lax.fori_loop(1, slots, one, 0)

    if last:
        valid = valid_rows((T, 1), bound, end_prev, end_cur)
        for h in range(H):
            mixed = acc[h, :, 0:D] / acc[h, :, D:2 * D]
            out[:, h * D:(h + 1) * D] = jnp.where(valid, mixed, 0.0).astype(BF16)


smem = pl.BlockSpec(memory_space=pltpu.SMEM)
vmem = pl.BlockSpec(memory_space=pltpu.VMEM)
hbm = pl.BlockSpec(memory_space=pltpu.HBM)


def shape(*dims, kind=F32):
    return jax.ShapeDtypeStruct(dims, kind)


def call(kernel, tables, operands, outs, scratch=(), room=12, given=vmem):
    return pl.pallas_call(
        kernel, in_specs=[smem] * tables + [given] * (len(operands) - tables),
        out_specs=[vmem] * len(outs), out_shape=list(outs), scratch_shapes=list(scratch),
        compiler_params=pltpu.CompilerParams(
            vmem_limit_bytes=room << 20),
    )(*operands)


def window(distance, rooms):
    pairs = []
    for room in range(rooms):
        base = room * SPAN
        for i in range(base, base + SPAN):
            j = i + distance
            if j <= base + SPAN and j < rooms * SPAN:
                pairs.append((i, j))
    return pairs


def per_device(lin_query, lin_key, lin_value, lin_gate, lin_decay, norm_gain,
               soft_query, soft_key, soft_value, starts, lengths):
    places = lax.axis_size("ctx")
    rooms = places // SPAN
    share = lax.axis_size("head")
    width = H * D
    piece = PAIR * D
    around = [[(i, i - i % ROW + (i + step) % ROW) for i in range(places)] for step in range(ROW)]
    onward = [(i, i + ROW) for i in range(places) if i % SPAN < ROW]
    next_room = [(i, i + 1) for i in range(SPAN - 1, places - 1, SPAN)]

    def send(x, pairs):
        return lax.ppermute(x, "ctx", pairs)

    packed = shape(piece + EXTRA, D, kind=BF16)

    pair = shape(T, 2 * D, kind=BF16)
    *slices, cum, cum_t, kv = call(
        state_kernel, 0,
        [pltpu.with_memory_space_constraint(x, pltpu.HBM) for x in
         (starts, lengths, lin_decay.T, lin_key, lin_value, soft_key, soft_value)],
        [packed] * ROW + [shape(T, H), shape(H, T), pair],
        [pltpu.SMEM(starts.shape, jnp.int32), pltpu.SMEM(lengths.shape, jnp.int32),
         pltpu.VMEM((H, T), F32), pltpu.VMEM((T, width), BF16), pltpu.VMEM((T, width), BF16),
         pltpu.VMEM((ROW, piece, D), BF16), pltpu.VMEM((ROW, EXTRA, D), BF16),
         pltpu.SemaphoreType.DMA((7,))], given=hbm)
    row = [slices[0]] + [send(slices[j], around[j]) for j in range(1, ROW)]

    intra, = call(intra_kernel, 2,
                  (starts, lengths, lin_query, lin_key, lin_value, cum, cum_t),
                  [shape(T, width)], [pltpu.VMEM((T, T), F32)])

    table = [pltpu.VMEM((ROW, piece, D), F32), pltpu.VMEM((ROW, 8 * PAIR, D), F32)]
    row_total, = call(row_kernel, 0, row, [shape(piece, D, kind=BF16)], table)
    above = send(row_total, onward)
    ready = call(
        prefix_kernel, 0, (*row, above), [shape(piece, D, kind=BF16)] * ROW,
        table + [pltpu.VMEM((ROW, piece, D), BF16)])
    before = [ready[0]] + [send(ready[j], around[j]) for j in range(1, ROW)]

    left, = call(pass_kernel, 0, (*slices, *before), [shape(ROW, piece, D, kind=BF16)])
    passed = send(left, next_room)

    far_kv = [send(kv, window(m, rooms)) for m in range(1, ROW + 1)]
    far_kv += [send(far_kv[ROW - 1], [(i + ROW, j) for i, j in window(m, rooms)])
               for m in range(ROW + 1, SPAN + 1)]

    heads, squares = call(
        carry_kernel, 2, (starts, lengths, lin_query, intra, *before, passed, cum),
        [shape(T, width), shape(8, T)], [pltpu.VMEM((ROW, piece, D), BF16)])
    step = 1
    others = jnp.zeros_like(squares)
    while step < share:
        if step > 1:
            squares = squares + others
        others = lax.ppermute(squares, "head", [(i, i ^ step) for i in range(share)])
        step *= 2

    held = [shape(H, T, D), shape(H, T, 2 * D)]
    room = [pltpu.VMEM((FAR + 1, T, D), BF16), pltpu.VMEM((FAR + 1, T, 2 * D), BF16),
            pltpu.VMEM((H, T, D), BF16)]
    asked = (starts, lengths, soft_query, kv)
    running = call(functools.partial(soft_kernel, low=1, last=False), 2,
                   (*asked, *far_kv[:FAR]), held, room, room=20)
    soft_out, = call(functools.partial(soft_kernel, low=FAR + 1, last=True), 2,
                     (*asked, *far_kv[FAR:], *running), [shape(T, width, kind=BF16)],
                     room + [pltpu.VMEM(x.shape, F32) for x in held], room=24)

    lin_out, = call(
        functools.partial(norm_kernel, features=width * share), 0,
        (heads, lin_gate, norm_gain.reshape(1, width), squares, others),
        [shape(T, width, kind=BF16)])
    return (lin_out, soft_out)


def solution(mesh):
    wide = P("ctx", "head")
    return jax.shard_map(
        per_device, mesh=mesh,
        in_specs=(wide, wide, wide, wide, wide, P("head"), wide, wide, wide, P(), P()),
        out_specs=(wide, wide), check_vma=False,
    )
```

```python
import functools
import jax
import jax.numpy as jnp
from jax import lax
from jax.experimental import pallas as pl
from jax.experimental.pallas import tpu as pltpu
from jax.sharding import PartitionSpec as P


T = 384
D = 128
H = 8
SPAN = 8
NEG = -1e30
FAR = 4
GROUP = 2
EPS = 1e-06
GONE = -1e5
ROW = 4
PAIR = H // ROW
EXTRA = 16
HI = lax.Precision.HIGHEST
F32 = jnp.float32
BF16 = jnp.bfloat16
NT = (((1,), (1,)), ((), ()))
TN = (((0,), (0,)), ((), ()))


def iota(shape, axis):
    return lax.broadcasted_iota(jnp.int32, shape, axis)


def marks(starts, lengths):
    device = lax.axis_index("ctx")
    room = device // SPAN
    place = device % SPAN
    first = device * T
    at_start = place == 0
    bound = jnp.where(at_start, starts[room] - first, 0)
    earlier = jnp.maximum(room - 1, 0)
    end_prev = jnp.where(at_start & (room > 0), starts[earlier] + lengths[earlier] - first, 0)
    end_cur = starts[room] + lengths[room] - first
    return room, place, bound, end_prev, end_cur


def valid_rows(shape, bound, end_prev, end_cur):
    rows = iota(shape, 0)
    return rows < jnp.where(rows < bound, end_prev, end_cur)


def state_kernel(starts_in, lengths_in, dec_in, key_in, value_in, soft_key, soft_value,
                 s0, s1, s2, s3, cum, cum_t, both,
                 starts, lengths, dec_t, key, value, pack, rest, sems):
    moves = ((dec_in, dec_t), (starts_in, starts), (lengths_in, lengths), (key_in, key),
             (value_in, value), (soft_key, both.at[:, 0:D]), (soft_value, both.at[:, D:2 * D]))
    copies = [pltpu.make_async_copy(a, b, sems.at[n]) for n, (a, b) in enumerate(moves)]
    for copy in copies:
        copy.start()
    for copy in copies[:3]:
        copy.wait()
    _, place, bound, _, end_cur = marks(starts, lengths)
    lower = (iota((T, T), 1) <= iota((T, T), 0)).astype(F32)
    dec = dec_t[...]
    col = lax.dot_general(lower, dec, NT, precision=HI, preferred_element_type=F32)
    cum[...] = col
    cum_t[...] = lax.dot_general(dec, lower, NT, precision=HI, preferred_element_type=F32)
    rows = iota((T, 1), 0)
    keep = (rows >= bound) & (rows < end_cur)
    last = col[T - 1:T, :]
    to_end = jnp.where(keep, jnp.exp(last - col), 0.0)
    total = jnp.where(place == 0, GONE, last)
    for copy in copies[3:]:
        copy.wait()
    for h in range(H):
        part = slice(h * D, (h + 1) * D)
        scaled = (key[:, part].astype(F32) * to_end[:, h:h + 1]).astype(BF16)
        state = lax.dot_general(scaled, value[:, part], TN, preferred_element_type=F32)
        pack[h // PAIR, (h % PAIR) * D:(h % PAIR + 1) * D, :] = state.astype(BF16)
    at = iota((EXTRA, D), 0)
    for w in range(ROW):
        table = jnp.zeros((EXTRA, D), F32)
        for j in range(PAIR):
            one = jnp.broadcast_to(total[:, w * PAIR + j:w * PAIR + j + 1], (EXTRA, D))
            a = one.astype(BF16).astype(F32)
            b = (one - a).astype(BF16).astype(F32)
            c = one - a - b
            for i, x in enumerate((a, b, c)):
                table = jnp.where(at == 3 * j + i, x, table)
        rest[w] = table.astype(BF16)
    x = place % ROW
    for step, out in enumerate((s0, s1, s2, s3)):
        w = (x + step) % ROW
        out[0:PAIR * D, :] = pack[w]
        out[PAIR * D:PAIR * D + EXTRA, :] = rest[w]


def log_decays(ref):
    table = ref[PAIR * D:PAIR * D + EXTRA, :].astype(F32)
    return [table[3 * j:3 * j + 1] + table[3 * j + 1:3 * j + 2] + table[3 * j + 2:3 * j + 3]
            for j in range(PAIR)]


def gather_row(own, r1, r2, r3, states, logs):
    x = (lax.axis_index("ctx") % SPAN) % ROW
    for step, ref in enumerate((own, r1, r2, r3)):
        w = (x - step + ROW) % ROW
        states[w] = ref[0:PAIR * D, :].astype(F32)
        for j, one in enumerate(log_decays(ref)):
            logs[w, 8 * j:8 * j + 8, :] = jnp.broadcast_to(one, (8, D))


def row_kernel(own, r1, r2, r3, kv, above_kv, out, both, states, logs):
    both[0:T, :] = kv[...]
    both[T:2 * T, :] = above_kv[...]
    gather_row(own, r1, r2, r3, states, logs)
    for j in range(PAIR):
        part = slice(j * D, (j + 1) * D)
        c = [logs[w, 8 * j:8 * j + 1, :] for w in range(ROW)]
        total = (states[3, part, :] + jnp.exp(c[3]) * states[2, part, :]
                 + jnp.exp(c[3] + c[2]) * states[1, part, :]
                 + jnp.exp(c[3] + c[2] + c[1]) * states[0, part, :])
        out[part, :] = total.astype(BF16)


def prefix_kernel(own, r1, r2, r3, above, p0, p1, p2, p3, states, logs, ready):
    gather_row(own, r1, r2, r3, states, logs)
    for j in range(PAIR):
        part = slice(j * D, (j + 1) * D)
        c = [logs[w, 8 * j:8 * j + 1, :] for w in range(ROW)]
        state = above[part, :].astype(F32)
        ready[0, part, :] = state.astype(BF16)
        state1 = states[0, part, :]
        ready[1, part, :] = (state1 + jnp.exp(c[0]) * state).astype(BF16)
        state2 = states[1, part, :] + jnp.exp(c[1]) * state1
        ready[2, part, :] = (state2 + jnp.exp(c[0] + c[1]) * state).astype(BF16)
        state3 = states[2, part, :] + jnp.exp(c[2]) * state2
        ready[3, part, :] = (state3 + jnp.exp(c[0] + c[1] + c[2]) * state).astype(BF16)
    x = (lax.axis_index("ctx") % SPAN) % ROW
    for step, out in enumerate((p0, p1, p2, p3)):
        out[...] = ready[(x + step) % ROW]


def pass_kernel(s0, s1, s2, s3, p0, p1, p2, p3, out):
    x = (lax.axis_index("ctx") % SPAN) % ROW
    entering = (p0, p3, p2, p1)
    for step, ref in enumerate((s0, s1, s2, s3)):
        w = (x + step) % ROW
        logs = log_decays(ref)
        for j in range(PAIR):
            part = slice(j * D, (j + 1) * D)
            state = (ref[part, :].astype(F32)
                     + jnp.exp(logs[j]) * entering[step][part, :].astype(F32))
            out[w, part, :] = state.astype(BF16)


def intra_kernel(starts, lengths, query, key, value, cum, cum_t, out, bias):
    _, _, bound, _, _ = marks(starts, lengths)
    t = iota((T, T), 0)
    i = iota((T, T), 1)
    seen = (i <= t) & ((i >= bound) | (t < bound))
    bias[...] = jnp.where(seen, 0.0, NEG)
    for h in range(H):
        lanes = slice(h * D, (h + 1) * D)
        for r in range(T // D):
            part = slice(r * D, (r + 1) * D)
            wide = (r + 1) * D
            scores = lax.dot_general(query[part, lanes], key[0:wide, lanes], NT,
                                     preferred_element_type=F32)
            gap = (cum[part, h:h + 1] - cum_t[h:h + 1, 0:wide]) + bias[part, 0:wide]
            weights = (scores * jnp.exp(gap)).astype(BF16)
            out[part, lanes] = jnp.dot(weights, value[0:wide, lanes], preferred_element_type=F32)


def carry_kernel(starts, lengths, query, intra, p0, p1, p2, p3, passed, cum, out, squares,
                 states):
    _, place, bound, end_prev, end_cur = marks(starts, lengths)
    x = place % ROW
    for step, ref in enumerate((p0, p1, p2, p3)):
        states[(x - step + ROW) % ROW] = ref[...]

    @pl.when(place == 0)
    def _():
        states[...] = passed[...]

    rows = iota((T, 1), 0)
    valid = rows < jnp.where(rows < bound, end_prev, end_cur)
    enters = (rows < jnp.where(place > 0, T, bound)) & valid
    enter = jnp.where(enters, jnp.exp(cum[...]), 0.0)
    live = jnp.where(valid, 1.0, 0.0)
    acc = jnp.zeros((T, D), F32)
    for h in range(H):
        lanes = slice(h * D, (h + 1) * D)
        state = states[h // PAIR, (h % PAIR) * D:(h % PAIR + 1) * D, :]
        carried = jnp.dot(query[:, lanes], state, preferred_element_type=F32)
        heads = intra[:, lanes] * live + enter[:, h:h + 1] * carried
        out[:, lanes] = heads
        acc += heads * heads
    squares[...] = lax.dot_general(jnp.ones((8, D), F32), acc, NT, precision=HI,
                                   preferred_element_type=F32)


def norm_kernel(heads, gate, gain, squares, others, out, *, features):
    pick = (iota((8, D), 0) == 0).astype(F32)
    sums = lax.dot_general(squares[...] + others[...], pick, TN, precision=HI,
                           preferred_element_type=F32)
    scale = lax.rsqrt(sums * (1.0 / features) + EPS)
    for h in range(heads.shape[1] // D):
        lanes = slice(h * D, (h + 1) * D)
        gated = jax.nn.sigmoid(gate[:, lanes].astype(F32))
        out[:, lanes] = (heads[:, lanes] * scale * gain[:, lanes] * gated).astype(BF16)


def soft_kernel(starts, lengths, query, own, *rest, low, last):
    far = rest[:FAR]
    if last:
        top_in, acc_in, out, keys, values, asks, top, acc = rest[FAR:]
        top[...] = top_in[...]
        acc[...] = acc_in[...]
    else:
        above_kv, top, acc, keys, values, asks = rest[FAR:]
    room, place, bound, end_prev, end_cur = marks(starts, lengths)
    tail = place == 0
    count = jnp.where(tail, jnp.where(room > 0, SPAN, 0), place)
    begin_room = jnp.where(tail, jnp.maximum(room - 1, 0), room)
    begin = starts[begin_room] - begin_room * SPAN * T
    factor = (D ** -0.5) * 1.4426950408889634
    ones = jnp.ones((T, D), BF16)
    first = low - 1

    def take(slot, ref, needed):
        @pl.when(needed)
        def _():
            keys[slot] = ref[:, 0:D]
            values[slot, :, 0:D] = ref[:, D:2 * D]
            values[slot, :, D:2 * D] = ones

    if not last:
        take(0, own, place >= 0)
        take(FAR, above_kv, (place >= FAR))
    for slot in range(1, FAR + 1):
        used = slot + low - 1 <= count
        if slot == FAR:
            used = used & tail
        take(slot, far[slot - 1].at[pl.ds(first // FAR * T, T), :], used)

    for h in range(H):
        asks[h] = query[:, h * D:(h + 1) * D]

    def attend(slot, size, hidden, fresh=False):
        k = keys[slot]
        v = values[slot]
        span = GROUP if size == T else 1
        many = span * size

        def ask(h):
            return lax.dot_general(asks[h:h + span, 0:size, :].reshape(many, D), k, NT,
                                   preferred_element_type=F32)

        ahead = ask(0)
        for h in range(0, H, span):
            x = ahead
            if h + span < H:
                ahead = ask(h + span)
            x = (x.reshape(span, size, T) + hidden[None]).reshape(many, T)
            parts = [x[:, j * D:(j + 1) * D] for j in range(T // D)]
            best = functools.reduce(jnp.maximum, parts)
            peak = jnp.broadcast_to(jnp.max(best, axis=1, keepdims=True), (many, D)) * factor
            if not fresh:
                old = top[h:h + span, 0:size, :].reshape(many, D)
                peak = jnp.maximum(old, peak)
                shrink = jnp.exp2(old - peak)
            top[h:h + span, 0:size, :] = peak.reshape(span, size, D)
            p = jnp.concatenate([jnp.exp2(y * factor - peak).astype(BF16) for y in parts], axis=1)
            mixed = jnp.dot(p, v, preferred_element_type=F32)
            if not fresh:
                kept = acc[h:h + span, 0:size, :].reshape(many, 2 * D)
                mixed = mixed + kept * jnp.concatenate([shrink, shrink], axis=1)
            acc[h:h + span, 0:size, :] = mixed.reshape(span, size, 2 * D)

    if low == 1:
        t = iota((T, T), 0)
        i = iota((T, T), 1)
        seen = (i <= t) & ((i >= bound) | (t < bound))
        attend(0, T, jnp.where(seen, 0.0, NEG), fresh=True)
    slots = jnp.minimum(count, low + FAR - 1) - low + 2

    def first_key(slot):
        return jnp.where(slot + low - 1 == count, begin, 0)

    @pl.when(place > 0)
    def _():
        def one(slot, _):
            attend(slot, T, jnp.where(iota((1, T), 1) < first_key(slot), NEG, 0.0))
            return 0

        lax.fori_loop(1, slots, one, 0)

    half = T // 2

    @pl.when(tail & (count > 0))
    def _():
        def one(slot, _):
            seen = (iota((half, T), 0) < bound) & (iota((half, T), 1) >= first_key(slot))
            attend(slot, half, jnp.where(seen, 0.0, NEG))
            return 0

        lax.fori_loop(1, slots, one, 0)

    if last:
        valid = valid_rows((T, 1), bound, end_prev, end_cur)
        for h in range(H):
            mixed = acc[h, :, 0:D] / acc[h, :, D:2 * D]
            out[:, h * D:(h + 1) * D] = jnp.where(valid, mixed, 0.0).astype(BF16)


smem = pl.BlockSpec(memory_space=pltpu.SMEM)
vmem = pl.BlockSpec(memory_space=pltpu.VMEM)
hbm = pl.BlockSpec(memory_space=pltpu.HBM)


def shape(*dims, kind=F32):
    return jax.ShapeDtypeStruct(dims, kind)


def call(kernel, tables, operands, outs, scratch=(), room=12, given=vmem):
    return pl.pallas_call(
        kernel, in_specs=[smem] * tables + [given] * (len(operands) - tables),
        out_specs=[vmem] * len(outs), out_shape=list(outs), scratch_shapes=list(scratch),
        compiler_params=pltpu.CompilerParams(
            vmem_limit_bytes=room << 20),
    )(*operands)


def window(distance, rooms):
    pairs = []
    for room in range(rooms):
        base = room * SPAN
        for i in range(base, base + SPAN):
            j = i + distance
            if j <= base + SPAN and j < rooms * SPAN:
                pairs.append((i, j))
    return pairs


def per_device(lin_query, lin_key, lin_value, lin_gate, lin_decay, norm_gain,
               soft_query, soft_key, soft_value, starts, lengths):
    places = lax.axis_size("ctx")
    rooms = places // SPAN
    share = lax.axis_size("head")
    width = H * D
    piece = PAIR * D
    around = [[(i, i - i % ROW + (i + step) % ROW) for i in range(places)] for step in range(ROW)]
    onward = [(i, i + ROW) for i in range(places) if i % SPAN < ROW]
    next_room = [(i, i + 1) for i in range(SPAN - 1, places - 1, SPAN)]

    def send(x, pairs):
        return lax.ppermute(x, "ctx", pairs)

    packed = shape(piece + EXTRA, D, kind=BF16)

    pair = shape(T, 2 * D, kind=BF16)
    *slices, cum, cum_t, kv = call(
        state_kernel, 0,
        [pltpu.with_memory_space_constraint(x, pltpu.HBM) for x in
         (starts, lengths, lin_decay.T, lin_key, lin_value, soft_key, soft_value)],
        [packed] * ROW + [shape(T, H), shape(H, T), pair],
        [pltpu.SMEM(starts.shape, jnp.int32), pltpu.SMEM(lengths.shape, jnp.int32),
         pltpu.VMEM((H, T), F32), pltpu.VMEM((T, width), BF16), pltpu.VMEM((T, width), BF16),
         pltpu.VMEM((ROW, piece, D), BF16), pltpu.VMEM((ROW, EXTRA, D), BF16),
         pltpu.SemaphoreType.DMA((7,))], given=hbm)
    row = [slices[0]] + [send(slices[j], around[j]) for j in range(1, ROW)]

    intra, = call(intra_kernel, 2,
                  (starts, lengths, lin_query, lin_key, lin_value, cum, cum_t),
                  [shape(T, width)], [pltpu.VMEM((T, T), F32)])

    table = [pltpu.VMEM((ROW, piece, D), F32), pltpu.VMEM((ROW, 8 * PAIR, D), F32)]
    above_kv = send(kv, onward)
    row_total, pair_kv = call(row_kernel, 0, (*row, kv, above_kv),
                              [shape(piece, D, kind=BF16), shape(2 * T, 2 * D, kind=BF16)], table)
    above = send(row_total, onward)
    ready = call(
        prefix_kernel, 0, (*row, above), [shape(piece, D, kind=BF16)] * ROW,
        table + [pltpu.VMEM((ROW, piece, D), BF16)])
    before = [ready[0]] + [send(ready[j], around[j]) for j in range(1, ROW)]

    left, = call(pass_kernel, 0, (*slices, *before), [shape(ROW, piece, D, kind=BF16)])
    passed = send(left, next_room)

    far_kv = [send(pair_kv, window(m, rooms)) for m in range(1, ROW)]
    far_kv += [send(pair_kv, [(i, i + ROW) for i in range(ROW, places - ROW, SPAN)])]

    heads, squares = call(
        carry_kernel, 2, (starts, lengths, lin_query, intra, *before, passed, cum),
        [shape(T, width), shape(8, T)], [pltpu.VMEM((ROW, piece, D), BF16)])
    step = 1
    others = jnp.zeros_like(squares)
    while step < share:
        if step > 1:
            squares = squares + others
        others = lax.ppermute(squares, "head", [(i, i ^ step) for i in range(share)])
        step *= 2

    held = [shape(H, T, D), shape(H, T, 2 * D)]
    room = [pltpu.VMEM((FAR + 1, T, D), BF16), pltpu.VMEM((FAR + 1, T, 2 * D), BF16),
            pltpu.VMEM((H, T, D), BF16)]
    asked = (starts, lengths, soft_query, kv)
    running = call(functools.partial(soft_kernel, low=1, last=False), 2,
                   (*asked, *far_kv, above_kv), held, room, room=20)
    soft_out, = call(functools.partial(soft_kernel, low=FAR + 1, last=True), 2,
                     (*asked, *far_kv, *running), [shape(T, width, kind=BF16)],
                     room + [pltpu.VMEM(x.shape, F32) for x in held], room=24)

    lin_out, = call(
        functools.partial(norm_kernel, features=width * share), 0,
        (heads, lin_gate, norm_gain.reshape(1, width), squares, others),
        [shape(T, width, kind=BF16)])
    return (lin_out, soft_out)


def solution(mesh):
    wide = P("ctx", "head")
    return jax.shard_map(
        per_device, mesh=mesh,
        in_specs=(wide, wide, wide, wide, wide, P("head"), wide, wide, wide, P(), P()),
        out_specs=(wide, wide), check_vma=False,
    )
```

```python
import functools
import jax
import jax.numpy as jnp
from jax import lax
from jax.experimental import pallas as pl
from jax.experimental.pallas import tpu as pltpu
from jax.sharding import PartitionSpec as P


T = 384
D = 128
H = 8
SPAN = 8
NEG = -1e30
FAR = 4
GROUP = 4
EPS = 1e-06
GONE = -1e5
ROW = 4
PAIR = H // ROW
EXTRA = 16
HI = lax.Precision.HIGHEST
F32 = jnp.float32
BF16 = jnp.bfloat16
NT = (((1,), (1,)), ((), ()))
TN = (((0,), (0,)), ((), ()))


def iota(shape, axis):
    return lax.broadcasted_iota(jnp.int32, shape, axis)


def marks(starts, lengths):
    device = lax.axis_index("ctx")
    room = device // SPAN
    place = device % SPAN
    first = device * T
    at_start = place == 0
    bound = jnp.where(at_start, starts[room] - first, 0)
    earlier = jnp.maximum(room - 1, 0)
    end_prev = jnp.where(at_start & (room > 0), starts[earlier] + lengths[earlier] - first, 0)
    end_cur = starts[room] + lengths[room] - first
    return room, place, bound, end_prev, end_cur


def valid_rows(shape, bound, end_prev, end_cur):
    rows = iota(shape, 0)
    return rows < jnp.where(rows < bound, end_prev, end_cur)


def state_kernel(starts_in, lengths_in, dec_in, key_in, value_in, soft_key, soft_value,
                 s0, s1, s2, s3, cum, cum_t, both,
                 starts, lengths, dec_t, key, value, pack, rest, sems):
    moves = ((dec_in, dec_t), (starts_in, starts), (lengths_in, lengths), (key_in, key),
             (value_in, value), (soft_key, both.at[:, 0:D]), (soft_value, both.at[:, D:2 * D]))
    copies = [pltpu.make_async_copy(a, b, sems.at[n]) for n, (a, b) in enumerate(moves)]
    for copy in copies:
        copy.start()
    for copy in copies[:3]:
        copy.wait()
    _, place, bound, _, end_cur = marks(starts, lengths)
    lower = (iota((T, T), 1) <= iota((T, T), 0)).astype(F32)
    dec = dec_t[...]
    col = lax.dot_general(lower, dec, NT, precision=HI, preferred_element_type=F32)
    cum[...] = col
    cum_t[...] = lax.dot_general(dec, lower, NT, precision=HI, preferred_element_type=F32)
    rows = iota((T, 1), 0)
    keep = (rows >= bound) & (rows < end_cur)
    last = col[T - 1:T, :]
    to_end = jnp.where(keep, jnp.exp(last - col), 0.0)
    total = jnp.where(place == 0, GONE, last)
    for copy in copies[3:]:
        copy.wait()
    for h in range(H):
        part = slice(h * D, (h + 1) * D)
        scaled = (key[:, part].astype(F32) * to_end[:, h:h + 1]).astype(BF16)
        state = lax.dot_general(scaled, value[:, part], TN, preferred_element_type=F32)
        pack[h // PAIR, (h % PAIR) * D:(h % PAIR + 1) * D, :] = state.astype(BF16)
    at = iota((EXTRA, D), 0)
    for w in range(ROW):
        table = jnp.zeros((EXTRA, D), F32)
        for j in range(PAIR):
            one = jnp.broadcast_to(total[:, w * PAIR + j:w * PAIR + j + 1], (EXTRA, D))
            a = one.astype(BF16).astype(F32)
            b = (one - a).astype(BF16).astype(F32)
            c = one - a - b
            for i, x in enumerate((a, b, c)):
                table = jnp.where(at == 3 * j + i, x, table)
        rest[w] = table.astype(BF16)
    x = place % ROW
    for step, out in enumerate((s0, s1, s2, s3)):
        w = (x + step) % ROW
        out[0:PAIR * D, :] = pack[w]
        out[PAIR * D:PAIR * D + EXTRA, :] = rest[w]


def log_decays(ref):
    table = ref[PAIR * D:PAIR * D + EXTRA, :].astype(F32)
    return [table[3 * j:3 * j + 1] + table[3 * j + 1:3 * j + 2] + table[3 * j + 2:3 * j + 3]
            for j in range(PAIR)]


def gather_row(own, r1, r2, r3, states, logs):
    x = (lax.axis_index("ctx") % SPAN) % ROW
    for step, ref in enumerate((own, r1, r2, r3)):
        w = (x - step + ROW) % ROW
        states[w] = ref[0:PAIR * D, :].astype(F32)
        for j, one in enumerate(log_decays(ref)):
            logs[w, 8 * j:8 * j + 8, :] = jnp.broadcast_to(one, (8, D))


def row_kernel(own, r1, r2, r3, out, states, logs):
    gather_row(own, r1, r2, r3, states, logs)
    at = iota((EXTRA, D), 0)
    table = jnp.zeros((EXTRA, D), F32)
    for j in range(PAIR):
        part = slice(j * D, (j + 1) * D)
        c = [logs[w, 8 * j:8 * j + 1, :] for w in range(ROW)]
        total = (states[3, part, :] + jnp.exp(c[3]) * states[2, part, :]
                 + jnp.exp(c[3] + c[2]) * states[1, part, :]
                 + jnp.exp(c[3] + c[2] + c[1]) * states[0, part, :])
        out[part, :] = total.astype(BF16)
        one = jnp.broadcast_to(c[0] + c[1] + c[2] + c[3], (EXTRA, D))
        a = one.astype(BF16).astype(F32)
        b = (one - a).astype(BF16).astype(F32)
        for i, x in enumerate((a, b, one - a - b)):
            table = jnp.where(at == 3 * j + i, x, table)
    out[PAIR * D:PAIR * D + EXTRA, :] = table.astype(BF16)


def prefix_kernel(own, r1, r2, r3, z1, z2, p0, p1, p2, p3, states, logs, ready):
    gather_row(own, r1, r2, r3, states, logs)
    decay = log_decays(z1)
    for j in range(PAIR):
        part = slice(j * D, (j + 1) * D)
        c = [logs[w, 8 * j:8 * j + 1, :] for w in range(ROW)]
        state = (z1[part, :].astype(F32) + jnp.exp(decay[j]) * z2[part, :].astype(F32))
        ready[0, part, :] = state.astype(BF16)
        state1 = states[0, part, :]
        ready[1, part, :] = (state1 + jnp.exp(c[0]) * state).astype(BF16)
        state2 = states[1, part, :] + jnp.exp(c[1]) * state1
        ready[2, part, :] = (state2 + jnp.exp(c[0] + c[1]) * state).astype(BF16)
        state3 = states[2, part, :] + jnp.exp(c[2]) * state2
        ready[3, part, :] = (state3 + jnp.exp(c[0] + c[1] + c[2]) * state).astype(BF16)
    x = (lax.axis_index("ctx") % SPAN) % ROW
    for step, out in enumerate((p0, p1, p2, p3)):
        out[...] = ready[(x + step) % ROW]


def intra_kernel(starts, lengths, query, key, value, cum, cum_t, out, bias):
    _, _, bound, _, _ = marks(starts, lengths)
    t = iota((T, T), 0)
    i = iota((T, T), 1)
    seen = (i <= t) & ((i >= bound) | (t < bound))
    bias[...] = jnp.where(seen, 0.0, NEG)
    for h in range(H):
        lanes = slice(h * D, (h + 1) * D)
        for r in range(T // D):
            part = slice(r * D, (r + 1) * D)
            wide = (r + 1) * D
            scores = lax.dot_general(query[part, lanes], key[0:wide, lanes], NT,
                                     preferred_element_type=F32)
            gap = (cum[part, h:h + 1] - cum_t[h:h + 1, 0:wide]) + bias[part, 0:wide]
            weights = (scores * jnp.exp(gap)).astype(BF16)
            out[part, lanes] = jnp.dot(weights, value[0:wide, lanes], preferred_element_type=F32)


def carry_kernel(starts, lengths, query, intra, p0, p1, p2, p3, cum, out, squares, states):
    _, place, bound, end_prev, end_cur = marks(starts, lengths)
    x = place % ROW
    for step, ref in enumerate((p0, p1, p2, p3)):
        states[(x - step + ROW) % ROW] = ref[...]
    rows = iota((T, 1), 0)
    valid = rows < jnp.where(rows < bound, end_prev, end_cur)
    enters = (rows < jnp.where(place > 0, T, bound)) & valid
    enter = jnp.where(enters, jnp.exp(cum[...]), 0.0)
    live = jnp.where(valid, 1.0, 0.0)
    acc = jnp.zeros((T, D), F32)
    for h in range(H):
        lanes = slice(h * D, (h + 1) * D)
        state = states[h // PAIR, (h % PAIR) * D:(h % PAIR + 1) * D, :]
        carried = jnp.dot(query[:, lanes], state, preferred_element_type=F32)
        heads = intra[:, lanes] * live + enter[:, h:h + 1] * carried
        out[:, lanes] = heads
        acc += heads * heads
    squares[...] = lax.dot_general(jnp.ones((8, D), F32), acc, NT, precision=HI,
                                   preferred_element_type=F32)


def norm_kernel(heads, gate, gain, squares, others, out, *, features):
    pick = (iota((8, D), 0) == 0).astype(F32)
    sums = lax.dot_general(squares[...] + others[...], pick, TN, precision=HI,
                           preferred_element_type=F32)
    scale = lax.rsqrt(sums * (1.0 / features) + EPS)
    for h in range(heads.shape[1] // D):
        lanes = slice(h * D, (h + 1) * D)
        gated = jax.nn.sigmoid(gate[:, lanes].astype(F32))
        out[:, lanes] = (heads[:, lanes] * scale * gain[:, lanes] * gated).astype(BF16)


def soft_kernel(starts, lengths, query, own, *rest, low, last):
    far = rest[:FAR]
    if last:
        top_in, acc_in, out, keys, values, asks, top, acc = rest[FAR:]
        top[...] = top_in[...]
        acc[...] = acc_in[...]
    else:
        top, acc, keys, values, asks = rest[FAR:]
    room, place, bound, end_prev, end_cur = marks(starts, lengths)
    tail = place == 0
    count = jnp.where(tail, jnp.where(room > 0, SPAN, 0), place)
    begin_room = jnp.where(tail, jnp.maximum(room - 1, 0), room)
    begin = starts[begin_room] - begin_room * SPAN * T
    factor = (D ** -0.5) * 1.4426950408889634
    ones = jnp.ones((T, D), BF16)
    for slot, ref in enumerate((own,) + far):
        @pl.when((slot + low - 1 <= count) if slot else (low == 1))
        def _():
            keys[slot] = ref[:, 0:D]
            values[slot, :, 0:D] = ref[:, D:2 * D]
            values[slot, :, D:2 * D] = ones

    for h in range(H):
        asks[h] = query[:, h * D:(h + 1) * D]

    def attend(slot, size, hidden, fresh=False):
        k = keys[slot]
        v = values[slot]
        span = GROUP if size == T else 1
        many = span * size

        def ask(h):
            return lax.dot_general(asks[h:h + span, 0:size, :].reshape(many, D), k, NT,
                                   preferred_element_type=F32)

        ahead = ask(0)
        for h in range(0, H, span):
            x = ahead
            if h + span < H:
                ahead = ask(h + span)
            if hidden is not None:
                x = (x.reshape(span, size, T) + hidden[None]).reshape(many, T)
            parts = [x[:, j * D:(j + 1) * D] for j in range(T // D)]
            best = functools.reduce(jnp.maximum, parts)
            peak = jnp.broadcast_to(jnp.max(best, axis=1, keepdims=True), (many, D)) * factor
            if not fresh:
                old = top[h:h + span, 0:size, :].reshape(many, D)
                peak = jnp.maximum(old, peak)
                shrink = jnp.exp2(old - peak)
            top[h:h + span, 0:size, :] = peak.reshape(span, size, D)
            p = jnp.concatenate([jnp.exp2(y * factor - peak).astype(BF16) for y in parts], axis=1)
            mixed = jnp.dot(p, v, preferred_element_type=F32)
            if not fresh:
                kept = acc[h:h + span, 0:size, :].reshape(many, 2 * D)
                mixed = mixed + kept * jnp.concatenate([shrink, shrink], axis=1)
            acc[h:h + span, 0:size, :] = mixed.reshape(span, size, 2 * D)

    if low == 1:
        t = iota((T, T), 0)
        i = iota((T, T), 1)
        seen = (i <= t) & ((i >= bound) | (t < bound))
        attend(0, T, jnp.where(seen, 0.0, NEG), fresh=True)
    slots = jnp.minimum(count, low + FAR - 1) - low + 2

    def first_key(slot):
        return jnp.where(slot + low - 1 == count, begin, 0)

    @pl.when(place > 0)
    def _():
        def one(slot, _):
            attend(slot, T, None)
            return 0

        farthest = count - low + 1
        lax.fori_loop(1, jnp.minimum(slots, farthest), one, 0)

        @pl.when((farthest >= 1) & (farthest < slots))
        def _():
            attend(farthest, T, jnp.where(iota((1, T), 1) < begin, NEG, 0.0))

    half = T // 2

    @pl.when(tail & (count > 0))
    def _():
        def one(slot, _):
            seen = (iota((half, T), 0) < bound) & (iota((half, T), 1) >= first_key(slot))
            attend(slot, half, jnp.where(seen, 0.0, NEG))
            return 0

        lax.fori_loop(1, slots, one, 0)

    if last:
        valid = valid_rows((T, 1), bound, end_prev, end_cur)
        for h in range(H):
            mixed = acc[h, :, 0:D] / acc[h, :, D:2 * D]
            out[:, h * D:(h + 1) * D] = jnp.where(valid, mixed, 0.0).astype(BF16)


smem = pl.BlockSpec(memory_space=pltpu.SMEM)
vmem = pl.BlockSpec(memory_space=pltpu.VMEM)
hbm = pl.BlockSpec(memory_space=pltpu.HBM)


def shape(*dims, kind=F32):
    return jax.ShapeDtypeStruct(dims, kind)


def call(kernel, tables, operands, outs, scratch=(), room=12, given=vmem):
    return pl.pallas_call(
        kernel, in_specs=[smem] * tables + [given] * (len(operands) - tables),
        out_specs=[vmem] * len(outs), out_shape=list(outs), scratch_shapes=list(scratch),
        compiler_params=pltpu.CompilerParams(
            vmem_limit_bytes=room << 20),
    )(*operands)


def window(distance, rooms):
    pairs = []
    for room in range(rooms):
        base = room * SPAN
        for i in range(base, base + SPAN):
            j = i + distance
            if j <= base + SPAN and j < rooms * SPAN:
                pairs.append((i, j))
    return pairs


def per_device(lin_query, lin_key, lin_value, lin_gate, lin_decay, norm_gain,
               soft_query, soft_key, soft_value, starts, lengths):
    places = lax.axis_size("ctx")
    rooms = places // SPAN
    share = lax.axis_size("head")
    width = H * D
    piece = PAIR * D
    around = [[(i, i - i % ROW + (i + step) % ROW) for i in range(places)] for step in range(ROW)]
    onward = [(i, i + ROW) for i in range(places - ROW)]
    beyond = [(i, i + 2 * ROW) for i in range(places - 2 * ROW) if i // ROW % 2 == 0]

    def send(x, pairs):
        return lax.ppermute(x, "ctx", pairs)

    packed = shape(piece + EXTRA, D, kind=BF16)

    pair = shape(T, 2 * D, kind=BF16)
    *slices, cum, cum_t, kv = call(
        state_kernel, 0,
        [pltpu.with_memory_space_constraint(x, pltpu.HBM) for x in
         (starts, lengths, lin_decay.T, lin_key, lin_value, soft_key, soft_value)],
        [packed] * ROW + [shape(T, H), shape(H, T), pair],
        [pltpu.SMEM(starts.shape, jnp.int32), pltpu.SMEM(lengths.shape, jnp.int32),
         pltpu.VMEM((H, T), F32), pltpu.VMEM((T, width), BF16), pltpu.VMEM((T, width), BF16),
         pltpu.VMEM((ROW, piece, D), BF16), pltpu.VMEM((ROW, EXTRA, D), BF16),
         pltpu.SemaphoreType.DMA((7,))], given=hbm)
    row = [slices[0]] + [send(slices[j], around[j]) for j in range(1, ROW)]

    intra, = call(intra_kernel, 2,
                  (starts, lengths, lin_query, lin_key, lin_value, cum, cum_t),
                  [shape(T, width)], [pltpu.VMEM((T, T), F32)])

    table = [pltpu.VMEM((ROW, piece, D), F32), pltpu.VMEM((ROW, 8 * PAIR, D), F32)]
    row_total, = call(row_kernel, 0, row, [packed], table)
    above = send(row_total, onward)
    above2 = send(row_total, beyond)
    ready = call(
        prefix_kernel, 0, (*row, above, above2), [shape(piece, D, kind=BF16)] * ROW,
        table + [pltpu.VMEM((ROW, piece, D), BF16)])
    before = [ready[0]] + [send(ready[j], around[j]) for j in range(1, ROW)]

    far_kv = [send(kv, window(m, rooms)) for m in range(1, ROW + 1)]
    far_kv += [send(far_kv[ROW - 1], [(i + ROW, j) for i, j in window(m, rooms)])
               for m in range(ROW + 1, SPAN + 1)]

    heads, squares = call(
        carry_kernel, 2, (starts, lengths, lin_query, intra, *before, cum),
        [shape(T, width), shape(8, T)], [pltpu.VMEM((ROW, piece, D), BF16)])
    step = 1
    others = jnp.zeros_like(squares)
    while step < share:
        if step > 1:
            squares = squares + others
        others = lax.ppermute(squares, "head", [(i, i ^ step) for i in range(share)])
        step *= 2

    held = [shape(H, T, D), shape(H, T, 2 * D)]
    room = [pltpu.VMEM((FAR + 1, T, D), BF16), pltpu.VMEM((FAR + 1, T, 2 * D), BF16),
            pltpu.VMEM((H, T, D), BF16)]
    asked = (starts, lengths, soft_query, kv)
    running = call(functools.partial(soft_kernel, low=1, last=False), 2,
                   (*asked, *far_kv[:FAR]), held, room, room=20)
    soft_out, = call(functools.partial(soft_kernel, low=FAR + 1, last=True), 2,
                     (*asked, *far_kv[FAR:], *running), [shape(T, width, kind=BF16)],
                     room + [pltpu.VMEM(x.shape, F32) for x in held], room=24)

    lin_out, = call(
        functools.partial(norm_kernel, features=width * share), 0,
        (heads, lin_gate, norm_gain.reshape(1, width), squares, others),
        [shape(T, width, kind=BF16)])
    return (lin_out, soft_out)


def solution(mesh):
    wide = P("ctx", "head")
    return jax.shard_map(
        per_device, mesh=mesh,
        in_specs=(wide, wide, wide, wide, wide, P("head"), wide, wide, wide, P(), P()),
        out_specs=(wide, wide), check_vma=False,
    )
```
